512 devices in a mesh: band: 16 (over y_hi, x, core), tm: 32 (over y_lo, z).
Axes of the slice: x: 4, y: 4 (y_hi: 2, y_lo: 2; y = y_hi * 2 + y_lo), z: 16, core: 2. Of those that a mesh axis runs over, the one named last changes fastest.
Arguments:
- spectrum: bfloat16 [64, 128, 65536], P(None, 'band', 'tm'), may hold values from -6 to 6
- w_freq: bfloat16 [5, 64, 8], replicated, may hold values from -1 to 1
- b_freq: float32 [64], replicated, may hold values from -3 to 3
- dilation: int32 [64], replicated, may hold values from 1 to 128, as said below
- w_time: float32 [3, 64], replicated, may hold values from -3 to 3
- b_time: float32 [64], replicated, may hold values from -3 to 3
- w_mix: bfloat16 [128, 128], replicated, may hold values from -0.5 to 0.5
- ln_gain: float32 [64], replicated, may hold values from 0.1 to 1.9
- w_up: bfloat16 [64, 256], replicated, may hold values from -0.75 to 0.75
- b_up: float32 [256], replicated, may hold values from -3 to 3
- w_down: bfloat16 [256, 64], replicated, may hold values from -0.375 to 0.375
- b_down: float32 [64], replicated, may hold values from -3 to 3
- epoch_lengths: int32 [32, 8], P('tm'), may hold values from 1 to 1024, 2048 in all within a row
Outputs:
- epoch_mean: float32 [256, 8192], P('tm', 'band')
- epoch_power: float32 [256, 8192], P('tm', 'band')
The draws below stay inside these ranges and needn't reach their ends.
Inputs may be any that keep to these rules, and one draw needn't show every extreme that they name: One channel has a dilation of exactly 128.
All inputs are finite; a program needn't handle non-finite values.
Results may differ from the reference program's by a relative error of at most 0.0015.
Values may be sent and summed in bfloat16 or wider, within the bound.
A program may use at most 64 MiB of HBM per device.

```python
import math
import jax
import jax.numpy as jnp
import numpy as np
from jax import lax

C = 64
F = 128
GROUPS = 8
KF = 5
HID = 256
T_DEV = 2048
EP = 8
DMAX = 128
FRAMES = 65536
BLOCKS = 32
EPOCHS = 256
N_TM = 32


def draw_dilation(key, part):
    spread = jax.random.randint(key, (C,), 1, DMAX + 1)
    chosen = jax.random.randint(jax.random.fold_in(key, 7), (), 0, C)
    return jnp.where(jnp.arange(C) == chosen, DMAX, spread).astype(jnp.int32)


def block_levels(stream_key, dims, shards, low, largest):
    loudness = 1.0
    for axis_at, blocks in shards:
        draws = jax.random.uniform(jax.random.fold_in(jax.random.fold_in(stream_key, 6), axis_at), (blocks,), jnp.float32, low / len(shards), largest / len(shards))
        loudness = loudness * jnp.repeat(jnp.exp(draws), dims[axis_at] // blocks).reshape((-1,) + (1,) * (len(dims) - 1 - axis_at))
    return loudness


def length_profile(number_of, total, reach, skew):
    loads = [(1 << 20) // math.isqrt(grade ** skew) + 1 for grade in range(2, number_of + 1)]
    spare, holding = total - reach - (number_of - 1), [1] * (number_of - 1)
    while spare > 0:
        free = [i for i in range(number_of - 1) if holding[i] < reach]
        whole, remaining = sum([loads[i] for i in free]), spare
        for i in free:
            more = min(reach - holding[i], max(1, remaining * loads[i] // whole), spare)
            holding[i] = holding[i] + more
            spare = spare - more
    return np.array([reach] + holding)


def uneven_parts(stream_key, amount, total, limit, lean):
    if amount == 2:
        one = jax.random.randint(stream_key, (), max(1, total - limit), min(limit, total - 1) + 1)
        return jnp.stack([one, total - one])
    tallies = jnp.asarray(length_profile(amount, total, limit, lean), jnp.int32)
    couples = (amount - 1) // 2
    giver, receiver = tallies[1:1 + 2 * couples:2], tallies[2:2 + 2 * couples:2]
    room = jnp.minimum(giver - 1, limit - receiver)
    moved = jax.random.randint(jax.random.fold_in(stream_key, 1), (couples,), 0, 1 << 20) % (room + 1)
    tallies = tallies.at[1:1 + 2 * couples:2].set(giver - moved).at[2:2 + 2 * couples:2].set(receiver + moved)
    return tallies[jax.random.permutation(jax.random.fold_in(stream_key, 2), amount)]


def normal_values(key, extent, deviation, reach, shards=(), kind=jnp.bfloat16):
    result = jax.random.normal(key, extent, jnp.float32) * deviation
    if len(shards) > 0:
        result = block_levels(key, extent, shards, -0.22, 0.18) * result
    return jnp.clip(result, min=-reach, max=reach).astype(kind)


def setup_inputs(seed: int = 0) -> dict:
    streams_of = jax.random.split(jax.random.key(seed), 14)
    return {
        "spectrum": normal_values(streams_of[0], (C, F, FRAMES), 1.0, 6.0, ((1, 16), (2, 32))),
        "w_freq": normal_values(streams_of[1], (KF, C, C // GROUPS), (KF * C // GROUPS) ** -0.5, 1.0),
        "b_freq": normal_values(streams_of[2], (C,), 0.5, 3.0, (), jnp.float32),
        "dilation": draw_dilation(jax.random.fold_in(streams_of[13], 71), 0),
        "w_time": normal_values(streams_of[4], (3, C), 0.6, 3.0, (), jnp.float32),
        "b_time": normal_values(streams_of[5], (C,), 0.5, 3.0, (), jnp.float32),
        "w_mix": normal_values(streams_of[6], (F, F), F ** -0.5, 0.5),
        "ln_gain": jnp.clip(1.0 + 0.18 * jax.random.normal(streams_of[7], (C,), jnp.float32), 0.1, 1.9),
        "w_up": normal_values(streams_of[8], (C, HID), C ** -0.5, 0.75),
        "b_up": normal_values(streams_of[9], (HID,), 0.5, 3.0, (), jnp.float32),
        "w_down": normal_values(streams_of[10], (HID, C), HID ** -0.5, 0.375),
        "b_down": normal_values(streams_of[11], (C,), 0.5, 3.0, (), jnp.float32),
        "epoch_lengths": jax.vmap(lambda own: uneven_parts(own, EP, T_DEV, T_DEV // 2, 2))(jax.random.split(streams_of[12], BLOCKS)).reshape((BLOCKS, EP)).astype(jnp.int32),
    }


def dilated(ext, dilation, w_time, b_time, pad, length):

    def one(chan, step, taps, shift):
        left = lax.dynamic_slice_in_dim(chan, (pad - step).astype(jnp.int32), length, 1).astype(jnp.float32)
        middle = chan[:, pad:pad + length].astype(jnp.float32)
        right = lax.dynamic_slice_in_dim(chan, (pad + step).astype(jnp.int32), length, 1).astype(jnp.float32)
        return taps[0] * left + taps[1] * middle + taps[2] * right + shift
    return jax.vmap(one)(ext, dilation, w_time.T, b_time).astype(jnp.bfloat16)

def reference(spectrum, w_freq, b_freq, dilation, w_time, b_time, w_mix, ln_gain, w_up, b_up, w_down, b_down, epoch_lengths):
    group_size = C // GROUPS
    kernel = w_freq.astype(jnp.float32).reshape(KF, GROUPS, group_size, group_size)
    width_win = T_DEV + 2 * DMAX

    def per_block(j):
        start = j * T_DEV
        frames = start - DMAX + jnp.arange(width_win, dtype=jnp.int32)
        index = jnp.clip(frames, 0, FRAMES - 1).astype(jnp.int32)
        window = jnp.take(spectrum, index, axis=2).astype(jnp.float32)
        window = jnp.pad(window, ((0, 0), (2, 2), (0, 0)))
        grouped = window.reshape(GROUPS, group_size, F + 4, width_win)
        total = jnp.zeros((GROUPS, group_size, F, width_win), jnp.float32)
        for tap in range(KF):
            total = total + jnp.einsum('gio,gift->goft', kernel[tap], grouped[:, :, tap:tap + F])
        pre = total.reshape(C, F, width_win) + b_freq[:, None, None]
        valid = (frames >= 0) & (frames < FRAMES)
        spectral = jnp.where(valid[None, None, :], jax.nn.gelu(pre, approximate=True), 0.0).astype(jnp.bfloat16)
        filtered = dilated(spectral, dilation, w_time, b_time, DMAX, T_DEV)
        filt32 = filtered.astype(jnp.float32)
        mixed = jnp.einsum('gf,cft->cgt', w_mix.astype(jnp.float32), filt32)
        mean = lax.optimization_barrier(jnp.mean(mixed, axis=0))
        var = lax.optimization_barrier(jnp.mean((mixed - mean) ** 2, axis=0))
        normed = ((mixed - mean) * lax.rsqrt(var + 1e-05) * ln_gain[:, None, None]).astype(jnp.bfloat16)
        hidden = jnp.einsum('ch,cft->hft', w_up.astype(jnp.float32), normed.astype(jnp.float32)) + b_up[:, None, None]
        hidden = jax.nn.gelu(hidden, approximate=True).astype(jnp.bfloat16)
        block_out = jnp.einsum('hc,hft->cft', w_down.astype(jnp.float32), hidden.astype(jnp.float32)) + b_down[:, None, None] + filt32
        row = epoch_lengths[j]
        ends = jnp.cumsum(row)
        starts = ends - row
        local = jnp.arange(T_DEV, dtype=jnp.int32)
        member = ((local[None, :] >= starts[:, None]) & (local[None, :] < ends[:, None])).astype(jnp.float32)
        sums = jnp.einsum('et,cft->efc', member, block_out, precision=lax.Precision.HIGHEST)
        squares = jnp.einsum('et,cft->efc', member, block_out * block_out, precision=lax.Precision.HIGHEST)
        lens = row.astype(jnp.float32)[:, None]
        return (sums.reshape(EP, F * C) / lens, squares.reshape(EP, F * C) / lens)
    means, powers = lax.map(per_block, jnp.arange(N_TM, dtype=jnp.int32))
    return (means.reshape(EPOCHS, F * C), powers.reshape(EPOCHS, F * C))
```

```python
import jax
import jax.numpy as jnp
from jax import lax
from jax.sharding import PartitionSpec as P


def padded_2(block, sides, width, periodic):
    for axis, dim in sides:
        count = lax.axis_size(axis)
        forward = [(i, i + 1) for i in range(count - 1)]
        if periodic:
            forward.append((count - 1, 0))
        backward = [(target, source) for source, target in forward]
        low = lax.ppermute(
            lax.slice_in_dim(block, block.shape[dim] - width, None, axis=dim), axis, forward
        )
        high = lax.ppermute(lax.slice_in_dim(block, 0, width, axis=dim), axis, backward)
        block = jnp.concatenate([low, block, high], axis=dim)
    return block


def dilated(ext, dilation, w_time, b_time, pad, length):

    def one(chan, step, taps, shift):
        left = lax.dynamic_slice_in_dim(chan, pad - step, length, 1).astype(jnp.float32)
        middle = chan[:, pad : pad + length].astype(jnp.float32)
        right = lax.dynamic_slice_in_dim(chan, pad + step, length, 1).astype(jnp.float32)
        return taps[0] * left + taps[1] * middle + taps[2] * right + shift

    return jax.vmap(one)(ext, dilation, w_time.T, b_time).astype(jnp.bfloat16)


def bin_filter(padded, w_freq, b_freq, bins):
    channels = w_freq.shape[1]
    group_size = w_freq.shape[2]
    tiled = jnp.tile(w_freq, (1, 1, channels // group_size))
    owner = jnp.arange(channels) // group_size
    keep = owner[:, None] == owner[None, :]
    blocks = jnp.where(keep[None], tiled, jnp.zeros_like(tiled))
    total = jnp.einsum(
        "co,cft->oft", blocks[0], padded[:, 0:bins], preferred_element_type=jnp.float32
    )
    for tap in range(1, w_freq.shape[0]):
        total = total + jnp.einsum(
            "co,cft->oft",
            blocks[tap],
            padded[:, tap : tap + bins],
            preferred_element_type=jnp.float32,
        )
    return jax.nn.gelu(total + b_freq[:, None, None], approximate=True).astype(jnp.bfloat16)


def on_device(
    spectrum,
    w_freq,
    b_freq,
    dilation,
    w_time,
    b_time,
    w_mix,
    ln_gain,
    w_up,
    b_up,
    w_down,
    b_down,
    epoch_lengths,
):
    channels = spectrum.shape[0]
    local_bins = spectrum.shape[1]
    block_frames = spectrum.shape[2]
    bands = lax.axis_size("band")
    piece = block_frames // bands
    all_bins = local_bins * bands
    reach = 128
    longer = padded_2(spectrum, (("tm", 2),), reach, False)
    padded = padded_2(longer, (("band", 1),), 2, False)
    spectral = bin_filter(padded, w_freq, b_freq, local_bins)
    tm = lax.axis_index("tm")
    frame = tm * block_frames - reach + jnp.arange(block_frames + 2 * reach, dtype=jnp.int32)
    inside = (frame >= 0) & (frame < lax.axis_size("tm") * block_frames)
    spectral = jnp.where(inside, spectral, jnp.zeros_like(spectral))
    filtered = dilated(spectral, dilation, w_time, b_time, reach, block_frames)
    parts = jnp.transpose(filtered.reshape(channels, local_bins, bands, piece), (2, 0, 1, 3))
    swapped = lax.all_to_all(parts, "band", split_axis=0, concat_axis=0, tiled=True)
    filtered = jnp.transpose(swapped, (1, 0, 2, 3)).reshape(channels, all_bins, piece)
    row = epoch_lengths[0]
    ends = jnp.cumsum(row)
    starts = ends - row
    frame_ids = lax.axis_index("band") * piece + jnp.arange(piece, dtype=jnp.int32)
    member = (
        (frame_ids[None, :] >= starts[:, None]) & (frame_ids[None, :] < ends[:, None])
    ).astype(jnp.float32)
    epochs_here = row.shape[0]
    bin_block = min(32, all_bins)

    def per_block(block_id):
        rows = lax.dynamic_slice_in_dim(w_mix, block_id * bin_block, bin_block, 0)
        mixed = jnp.einsum("gf,cfp->cgp", rows, filtered, preferred_element_type=jnp.float32)
        mean = jnp.mean(mixed, axis=0)
        var = jnp.mean((mixed - mean) ** 2, axis=0)
        normed = ((mixed - mean) * lax.rsqrt(var + 1e-05) * ln_gain[:, None, None]).astype(
            jnp.bfloat16
        )
        flat = normed.reshape(channels, bin_block * piece)
        hidden = (
            jnp.einsum("ch,cn->hn", w_up, flat, preferred_element_type=jnp.float32) + b_up[:, None]
        )
        hidden = jax.nn.gelu(hidden, approximate=True).astype(jnp.bfloat16)
        projected = (
            jnp.einsum("hc,hn->cn", w_down, hidden, preferred_element_type=jnp.float32)
            + b_down[:, None]
        )
        resid = lax.dynamic_slice_in_dim(filtered, block_id * bin_block, bin_block, 1).astype(
            jnp.float32
        )
        block_out = projected.reshape(channels, bin_block, piece) + resid
        sums = jnp.einsum("et,cft->efc", member, block_out, precision=lax.Precision.HIGHEST)
        squares = jnp.einsum(
            "et,cft->efc", member, block_out * block_out, precision=lax.Precision.HIGHEST
        )
        return (sums, squares)

    sums, squares = lax.map(per_block, jnp.arange(all_bins // bin_block, dtype=jnp.int32))
    sums = jnp.transpose(sums, (1, 0, 2, 3)).reshape(epochs_here, all_bins * channels)
    squares = jnp.transpose(squares, (1, 0, 2, 3)).reshape(epochs_here, all_bins * channels)
    both = jnp.stack([sums, squares]).reshape(2, epochs_here, bands, local_bins * channels)
    both = lax.all_to_all(
        jnp.transpose(both, (2, 0, 1, 3)), "band", split_axis=0, concat_axis=0, tiled=True
    )
    total_sums, total_squares = jnp.sum(both, axis=0)
    lens = row.astype(jnp.float32)[:, None]
    return (total_sums / lens, total_squares / lens)


def solution(mesh):
    return jax.shard_map(
        on_device,
        mesh=mesh,
        in_specs=(
            P(None, "band", "tm"),
            P(),
            P(),
            P(),
            P(),
            P(),
            P(),
            P(),
            P(),
            P(),
            P(),
            P(),
            P("tm", None),
        ),
        out_specs=(P("tm", "band"), P("tm", "band")),
        check_vma=False,
    )
```

```python
import functools

import jax
import jax.numpy as jnp
import numpy as np
from jax import lax
from jax.experimental import pallas as pl
from jax.experimental.pallas import tpu as pltpu
from jax.sharding import PartitionSpec as P

REACH = 128
SUB = 8
GELU_C = 0.7978845608028654
GELU_A = 0.044715


def gelu(x):
    inner = x * (GELU_C + (GELU_C * GELU_A) * (x * x))
    half = 0.5 * x
    return half + half * jnp.tanh(inner)


def shifted(block, axis, step, periodic=False):
    count = lax.axis_size(axis)
    pairs = [(i, i + step) for i in range(count) if 0 <= i + step < count]
    return lax.ppermute(block, axis, pairs)


def banded_weights(w_freq, bins):
    taps, channels, size = w_freq.shape
    half = taps // 2
    place = np.zeros((taps, bins, bins + 2 * half), np.float32)
    for tap in range(taps):
        for f in range(bins):
            place[tap, f, f + tap] = 1
    grouped = w_freq.reshape(taps, channels // size, size, size)
    full = jnp.einsum(
        "kfp,kgco->gfocp",
        jnp.asarray(place, jnp.bfloat16),
        grouped,
        preferred_element_type=jnp.float32,
    ).astype(jnp.bfloat16)
    rows = bins * size
    own = full[..., half : half + bins].reshape(channels // size, rows, size * bins)
    low = full[..., :half].reshape(channels // size, rows, size * half)
    high = full[..., half + bins :].reshape(channels // size, rows, size * half)
    return jnp.concatenate([own, low, high], axis=2)


def front_kernel(bands, own_ref, low_ref, high_ref, w_ref, b_ref, taps_ref, dil_ref, flag_ref, out_ref, spec_ref):
    rows, long = own_ref.shape
    tiles = long // 128
    data = jnp.concatenate([own_ref[...], low_ref[...], high_ref[...]], axis=0)
    pre = jnp.dot(w_ref[0], data, preferred_element_type=jnp.float32)
    for j in range(tiles):
        cols = slice(j * 128, (j + 1) * 128)
        act = gelu(pre[:, cols] + b_ref[0])
        if j == 0:
            act = act * flag_ref[0, 0:1]
        if j == tiles - 1:
            act = act * flag_ref[1, 0:1]
        spec_ref[:, cols] = act.astype(jnp.bfloat16).astype(jnp.float32)
    step = dil_ref[0]
    lane = lax.broadcasted_iota(jnp.int32, (SUB, 128), 1)
    from_left = (lane - step) & 127
    from_right = (lane + step) & 127
    keep_left = lane >= step
    keep_right = lane + step < 128
    t0, t1, t2, shift = (taps_ref[0, i] for i in range(4))

    def take(value, index):
        return jnp.take_along_axis(value, index, axis=1, mode="promise_in_bounds")

    def half(start):
        v = [spec_ref[pl.ds(start, SUB), j * 128 : (j + 1) * 128] for j in range(tiles)]
        left = [take(v[j], from_left) for j in range(tiles - 1)]
        right = [take(v[j], from_right) for j in range(1, tiles)]
        outs = []
        for j in range(1, tiles - 1):
            a = jnp.where(keep_left, left[j], left[j - 1])
            c = jnp.where(keep_right, right[j - 1], right[j])
            outs.append(t0 * a + t1 * v[j] + t2 * c + shift)
        return outs

    for pair in range(rows // 16):
        top = half(pair * 16)
        bottom = half(pair * 16 + SUB)
        for j in range(bands):
            both = jnp.concatenate([top[j], bottom[j]], axis=0)
            out_ref[j, pair * 16 : (pair + 1) * 16, :] = both.astype(jnp.bfloat16)


def front(own, low, high, weights, bias, taps, dil, flags, bands):
    groups, rows, deep = weights.shape
    long = own.shape[1]
    side = low.shape[0] // groups
    return pl.pallas_call(
        functools.partial(front_kernel, bands),
        grid=(groups,),
        out_shape=jax.ShapeDtypeStruct((bands, rows, groups * 128), jnp.bfloat16),
        in_specs=[
            pl.BlockSpec((rows, long), lambda g: (g, 0)),
            pl.BlockSpec((side, long), lambda g: (g, 0)),
            pl.BlockSpec((side, long), lambda g: (g, 0)),
            pl.BlockSpec((1, rows, deep), lambda g: (g, 0, 0)),
            pl.BlockSpec((1, rows, 128), lambda g: (g, 0, 0)),
            pl.BlockSpec((1, 4, SUB, 128), lambda g: (g, 0, 0, 0)),
            pl.BlockSpec((1, SUB, 128), lambda g: (g, 0, 0)),
            pl.BlockSpec((2, SUB, 128), lambda g: (0, 0, 0)),
        ],
        out_specs=pl.BlockSpec((bands, rows, 128), lambda g: (0, 0, g)),
        scratch_shapes=[pltpu.VMEM((rows, long), jnp.float32)],
        name="front",
    )(own, low, high, weights, bias, taps, dil, flags)


def build_kron(mix_ref, kron_ref):
    size = kron_ref.shape[0]
    bins = size // SUB
    one = (
        lax.broadcasted_iota(jnp.int32, (size, bins), 0) // SUB
        == lax.broadcasted_iota(jnp.int32, (size, bins), 1)
    ).astype(jnp.bfloat16)
    tall = jnp.dot(one, mix_ref[...], preferred_element_type=jnp.float32).astype(jnp.bfloat16)
    wide = (
        lax.broadcasted_iota(jnp.int32, (bins, size), 1) // SUB
        == lax.broadcasted_iota(jnp.int32, (bins, size), 0)
    ).astype(jnp.bfloat16)
    kron_ref[...] = jnp.zeros_like(kron_ref)
    step = 256
    rows = lax.broadcasted_iota(jnp.int32, (step, step), 0)
    cols = lax.broadcasted_iota(jnp.int32, (step, step), 1)
    same = (rows % SUB) == (cols % SUB)
    for i in range(size // step):
        for j in range(size // step):
            part = jnp.dot(
                tall[i * step : (i + 1) * step],
                wide[:, j * step : (j + 1) * step],
                preferred_element_type=jnp.float32,
            )
            kron_ref[i * step : (i + 1) * step, j * step : (j + 1) * step] = jnp.where(
                same, part, 0.0
            ).astype(jnp.bfloat16)


def stacked(tile, groups, row):
    return jnp.concatenate(
        [tile[row * SUB : (row + 1) * SUB, g * 128 : (g + 1) * 128] for g in range(groups)], axis=0
    )


def back_chunk(chunk, some, groups, data_ref, mixed_ref, up_ref, bup_ref, down_ref, bdown_ref, gain_ref, member_ref, out_ref):
    channels = groups * SUB
    rows = some * SUB
    base = pl.multiple_of(chunk * rows, rows)
    mixed = mixed_ref[pl.ds(base, rows), :]
    normed = []
    for r in range(some):
        m = stacked(mixed, groups, r)
        dev = m - jnp.sum(m, axis=0, keepdims=True) * (1.0 / channels)
        var = jnp.sum(dev * dev, axis=0, keepdims=True) * (1.0 / channels)
        normed.append((dev * lax.rsqrt(var + 1e-05) * gain_ref[...]).astype(jnp.bfloat16))
    flat = jnp.concatenate(normed, axis=1)
    hidden = jnp.dot(up_ref[...], flat, preferred_element_type=jnp.float32)
    act = jnp.concatenate(
        [
            gelu(hidden[:, r * 128 : (r + 1) * 128] + bup_ref[...]).astype(jnp.bfloat16)
            for r in range(some)
        ],
        axis=1,
    )
    proj = jnp.dot(down_ref[...], act, preferred_element_type=jnp.float32)
    data = data_ref[pl.ds(base, rows), :].astype(jnp.float32)
    plain, square = [], []
    for r in range(some):
        block = proj[:, r * 128 : (r + 1) * 128] + bdown_ref[...] + stacked(data, groups, r)
        for value, store in ((block, plain), (block * block, square)):
            head = value.astype(jnp.bfloat16)
            tail = (value - head.astype(jnp.float32)).astype(jnp.bfloat16)
            store.append(jnp.concatenate([head, tail], axis=1))
    for k, store in enumerate((plain, square)):
        total = lax.dot_general(
            member_ref[...],
            jnp.concatenate(store, axis=0),
            (((1,), (1,)), ((), ())),
            preferred_element_type=jnp.float32,
        )
        out_ref[chunk, k] = total


def back_kernel(groups, some, data_ref, mix_ref, up_ref, bup_ref, down_ref, bdown_ref, gain_ref, member_ref, out_ref, kron_ref, mixed_ref):
    build_kron(mix_ref, kron_ref)
    size = kron_ref.shape[0]
    step = 128

    @pl.loop(0, size // step)
    def _(i):
        at = pl.multiple_of(i * step, step)
        mixed_ref[pl.ds(at, step), :] = jnp.dot(
            kron_ref[pl.ds(at, step), :], data_ref[...], preferred_element_type=jnp.float32
        )

    @pl.loop(0, size // (SUB * some))
    def _(chunk):
        back_chunk(chunk, some, groups, data_ref, mixed_ref, up_ref, bup_ref, down_ref, bdown_ref, gain_ref, member_ref, out_ref)


def back(data, w_mix, up, bup, down, bdown, gain, member, groups, some):
    size = data.shape[0]
    epochs = member.shape[0]
    bins = size // SUB
    channels = groups * SUB
    return pl.pallas_call(
        functools.partial(back_kernel, groups, some),
        out_shape=jax.ShapeDtypeStruct((bins // some, 2, epochs, some * channels), jnp.float32),
        in_specs=[pl.BlockSpec(memory_space=pltpu.VMEM)] * 8,
        out_specs=pl.BlockSpec(memory_space=pltpu.VMEM),
        scratch_shapes=[
            pltpu.VMEM((size, size), jnp.bfloat16),
            pltpu.VMEM((size, data.shape[1]), jnp.float32),
        ],
        name="back",
    )(data, w_mix, up, bup, down, bdown, gain, member)


def on_device(
    spectrum,
    w_freq,
    b_freq,
    dilation,
    w_time,
    b_time,
    w_mix,
    ln_gain,
    w_up,
    b_up,
    w_down,
    b_down,
    epoch_lengths,
):
    channels, bins, frames = spectrum.shape
    size = w_freq.shape[2]
    groups = channels // size
    bands = lax.axis_size("band")
    blocks = lax.axis_size("tm")
    tm = lax.axis_index("tm")
    long = frames + 2 * REACH
    some = bins // 2

    before = shifted(spectrum[:, :, frames - REACH :], "tm", 1)
    after = shifted(spectrum[:, :, :REACH], "tm", -1)
    longer = jnp.concatenate([before, spectrum, after], axis=2)
    low = shifted(longer[:, bins - 2 :], "band", 1).reshape(channels * 2, long)
    high = shifted(longer[:, :2], "band", -1).reshape(channels * 2, long)
    own = longer.reshape(channels * bins, long)

    weights = banded_weights(w_freq, bins)
    bias = jnp.broadcast_to(
        b_freq.reshape(groups, 1, size, 1), (groups, bins, size, 128)
    ).reshape(groups, bins * size, 128)
    taps = jnp.concatenate([w_time, b_time[None]], axis=0).reshape(4, groups, size, 1)
    taps = jnp.broadcast_to(jnp.transpose(taps, (1, 0, 2, 3)), (groups, 4, size, 128))
    dil = jnp.broadcast_to(dilation.reshape(groups, size, 1), (groups, size, 128))
    inside = jnp.stack([tm > 0, tm < blocks - 1]).astype(jnp.float32)
    flags = jnp.broadcast_to(inside[:, None, None], (2, SUB, 128))
    parts = front(own, low, high, weights, bias, taps, dil, flags, bands)

    swapped = lax.all_to_all(parts, "band", split_axis=0, concat_axis=0, tiled=True)
    data = swapped.reshape(bands * bins * size, groups * 128)

    row = epoch_lengths[0]
    epochs = row.shape[0]
    ends = jnp.cumsum(row)
    starts = ends - row
    piece = frames // bands
    ids = lax.axis_index("band") * piece + jnp.arange(piece, dtype=jnp.int32)
    member = ((ids[None, :] >= starts[:, None]) & (ids[None, :] < ends[:, None])).astype(jnp.bfloat16)
    member = jnp.concatenate([member, member], axis=1)

    def wide(x):
        return jnp.broadcast_to(x[:, None], (x.shape[0], 128))

    sums = back(data, w_mix, w_up.T, wide(b_up), w_down.T, wide(b_down), wide(ln_gain), member, groups, some)
    split = sums.reshape(bands, 2, 2, epochs, some * channels)
    got = lax.all_to_all(split, "band", split_axis=0, concat_axis=0, tiled=True)
    total = jnp.sum(got, axis=0) / row.astype(jnp.float32)[None, None, :, None]
    total = jnp.transpose(total, (1, 2, 0, 3)).reshape(2, epochs, bins * channels)
    return total[0], total[1]


def solution(mesh):
    return jax.shard_map(
        on_device,
        mesh=mesh,
        in_specs=(
            P(None, "band", "tm"),
            P(),
            P(),
            P(),
            P(),
            P(),
            P(),
            P(),
            P(),
            P(),
            P(),
            P(),
            P("tm", None),
        ),
        out_specs=(P("tm", "band"), P("tm", "band")),
        check_vma=False,
    )
```

```python
import functools

import jax
import jax.numpy as jnp
from jax import lax
from jax.experimental import pallas as pl
from jax.experimental.pallas import tpu as pltpu
from jax.sharding import PartitionSpec as P

MESH = pl.DeviceIdType.MESH
REACH = 128
SUB = 8
GELU_C = 0.7978845608028654
GELU_A = 0.044715


def gelu(x):
    inner = x * (GELU_C + (GELU_C * GELU_A) * (x * x))
    half = 0.5 * x
    return half + half * jnp.tanh(inner)


def build_kron(mix_ref, kron_ref):
    size = kron_ref.shape[0]
    bins = size // SUB
    one = (
        lax.broadcasted_iota(jnp.int32, (size, bins), 0) // SUB
        == lax.broadcasted_iota(jnp.int32, (size, bins), 1)
    ).astype(jnp.bfloat16)
    tall = jnp.dot(one, mix_ref[...], preferred_element_type=jnp.float32).astype(jnp.bfloat16)
    wide = (
        lax.broadcasted_iota(jnp.int32, (bins, size), 1) // SUB
        == lax.broadcasted_iota(jnp.int32, (bins, size), 0)
    ).astype(jnp.bfloat16)
    kron_ref[...] = jnp.zeros_like(kron_ref)
    step = 256
    rows = lax.broadcasted_iota(jnp.int32, (step, step), 0)
    cols = lax.broadcasted_iota(jnp.int32, (step, step), 1)
    same = (rows % SUB) == (cols % SUB)
    for i in range(size // step):
        for j in range(size // step):
            part = jnp.dot(
                tall[i * step : (i + 1) * step],
                wide[:, j * step : (j + 1) * step],
                preferred_element_type=jnp.float32,
            )
            kron_ref[i * step : (i + 1) * step, j * step : (j + 1) * step] = jnp.where(
                same, part, 0.0
            ).astype(jnp.bfloat16)


def stacked3(tile, groups, row):
    return jnp.concatenate([tile[g, row * SUB : (row + 1) * SUB, :] for g in range(groups)], axis=0)


def stacked(tile, groups, row):
    return jnp.concatenate(
        [tile[row * SUB : (row + 1) * SUB, g * 128 : (g + 1) * 128] for g in range(groups)], axis=0
    )


def back_chunk(chunk, some, groups, data_ref, mixed_ref, up_ref, bup_ref, down_ref, bdown_ref, gain_ref, member_ref):
    channels = groups * SUB
    rows = some * SUB
    base = pl.multiple_of(chunk * rows, rows)
    mixed = mixed_ref[pl.ds(base, rows), :]
    normed = []
    for r in range(some):
        m = stacked(mixed, groups, r)
        dev = m - jnp.sum(m, axis=0, keepdims=True) * (1.0 / channels)
        var = jnp.sum(dev * dev, axis=0, keepdims=True) * (1.0 / channels)
        normed.append((dev * lax.rsqrt(var + 1e-05) * gain_ref[...]).astype(jnp.bfloat16))
    flat = jnp.concatenate(normed, axis=1)
    hidden = jnp.dot(up_ref[...], flat, preferred_element_type=jnp.float32)
    act = jnp.concatenate(
        [
            gelu(hidden[:, r * 128 : (r + 1) * 128] + bup_ref[...]).astype(jnp.bfloat16)
            for r in range(some)
        ],
        axis=1,
    )
    proj = jnp.dot(down_ref[...], act, preferred_element_type=jnp.float32)
    data = data_ref[:, pl.ds(base, rows), :].astype(jnp.float32)
    plain, square = [], []
    for r in range(some):
        block = proj[:, r * 128 : (r + 1) * 128] + bdown_ref[...] + stacked3(data, groups, r)
        for value, store in ((block, plain), (block * block, square)):
            head = value.astype(jnp.bfloat16)
            tail = (value - head.astype(jnp.float32)).astype(jnp.bfloat16)
            store.append(jnp.concatenate([head, tail], axis=1))
    return [
        lax.dot_general(
            member_ref[...],
            jnp.concatenate(store, axis=0),
            (((1,), (1,)), ((), ())),
            preferred_element_type=jnp.float32,
        )
        for store in (plain, square)
    ]


def column(row, first, count):
    lane = lax.broadcasted_iota(jnp.int32, (count, row.shape[1]), 1)
    sub = lax.broadcasted_iota(jnp.int32, (count, row.shape[1]), 0)
    picked = jnp.where(lane == sub + first, jnp.broadcast_to(row, lane.shape), 0.0)
    return jnp.sum(picked, axis=1, keepdims=True)


def wide(col):
    return jnp.broadcast_to(col, (col.shape[0], 128))


def edge_picker(bins):
    shape = (4 * SUB, SUB * bins)
    row = lax.broadcasted_iota(jnp.int32, shape, 0)
    col = lax.broadcasted_iota(jnp.int32, shape, 1)
    edge = row % 2 + jnp.where(row >= 2 * SUB, bins - 2, 0)
    channel = (row % (2 * SUB)) // 2
    return (col == channel * bins + edge).astype(jnp.bfloat16)


def group_weights(wt_ref, g, bins, low_on, high_on):
    taps, size, channels = wt_ref.shape
    long = bins + taps - 1
    row = lax.broadcasted_iota(jnp.int32, (channels, 128), 0)
    q = lax.broadcasted_iota(jnp.int32, (channels, 128), 1)
    pick = ((row == g * size + q // long) & (q < size * long)).astype(jnp.bfloat16)
    spread = [
        jnp.dot(wt_ref[k], pick, preferred_element_type=jnp.float32) for k in range(taps)
    ]
    place = lax.broadcasted_iota(jnp.int32, (size, 128), 1) % long
    base = jnp.zeros((size, 128), jnp.float32)
    for k in range(taps):
        base = jnp.where(place == k, spread[k], base)
    turned = [base] + [pltpu.roll(base, f, 1) for f in range(1, bins)]
    big = jnp.concatenate(turned, axis=0).astype(jnp.bfloat16)
    wid = size * long
    p = lax.broadcasted_iota(jnp.int32, (128, wid), 1)
    src = lax.broadcasted_iota(jnp.int32, (128, wid), 0)
    inner = size * bins
    lo = p - inner
    hi = lo - 2 * size
    wanted = jnp.where(
        p < inner,
        (p // bins) * long + p % bins + 2,
        jnp.where(
            lo < 2 * size,
            (lo // 2) * long + lo % 2 + jnp.where(low_on, 0, 4096),
            (hi // 2) * long + bins + 2 + hi % 2 + jnp.where(high_on, 0, 4096),
        ),
    )
    order = (src == wanted).astype(jnp.bfloat16)
    return jnp.dot(big, order, preferred_element_type=jnp.float32).astype(jnp.bfloat16)


def front_group(g, bands, weights, own_ref, ends_ref, low_ref, high_ref, cor_ref, rows_of, before_on, after_on, spec_ref, send_ref):
    rows = weights.shape[0]
    long = own_ref.shape[1]
    tiles = long // 128 + 2
    at = pl.multiple_of(g * rows, rows)
    small = pl.multiple_of(g * 16, 16)
    body = jnp.concatenate(
        [own_ref[pl.ds(at, rows), :], low_ref[pl.ds(small, 16), :], high_ref[pl.ds(small, 16), :]],
        axis=0,
    )
    first, last = (
        jnp.concatenate(
            [
                ends_ref[i, pl.ds(at, rows), :],
                cor_ref[i, 0, pl.ds(small, 16), :],
                cor_ref[i, 1, pl.ds(small, 16), :],
            ],
            axis=0,
        )
        for i in range(2)
    )
    data = jnp.concatenate([first, body, last], axis=1)
    pre = jnp.dot(weights, data, preferred_element_type=jnp.float32)
    t0, t1, t2, shift, bias8, step = (wide(column(r, g * SUB, SUB)) for r in rows_of)
    bias = jnp.concatenate([bias8] * (rows // SUB), axis=0)
    step = step.astype(jnp.int32)
    for j in range(tiles):
        cols = slice(j * 128, (j + 1) * 128)
        act = gelu(pre[:, cols] + bias)
        if j == 0:
            act = act * before_on
        if j == tiles - 1:
            act = act * after_on
        spec_ref[:, cols] = act.astype(jnp.bfloat16).astype(jnp.float32)
    lane = lax.broadcasted_iota(jnp.int32, (SUB, 128), 1)
    from_left = (lane - step) & 127
    from_right = (lane + step) & 127
    keep_left = lane >= step
    keep_right = lane + step < 128

    def take(value, index):
        return jnp.take_along_axis(value, index, axis=1, mode="promise_in_bounds")

    def half(start):
        v = [spec_ref[start : start + SUB, j * 128 : (j + 1) * 128] for j in range(tiles)]
        left = [take(v[j], from_left) for j in range(tiles - 1)]
        right = [take(v[j], from_right) for j in range(1, tiles)]
        outs = []
        for j in range(1, tiles - 1):
            a = jnp.where(keep_left, left[j], left[j - 1])
            c = jnp.where(keep_right, right[j - 1], right[j])
            outs.append(t0 * a + t1 * v[j] + t2 * c + shift)
        return outs

    for pair in range(rows // 16):
        top = half(pair * 16)
        bottom = half(pair * 16 + SUB)
        for j in range(bands):
            both = jnp.concatenate([top[j], bottom[j]], axis=0)
            send_ref[g, j, pair * 16 : (pair + 1) * 16, :] = both.astype(jnp.bfloat16)


def kernel(
    bands,
    blocks,
    bins,
    some,
    own_ref,
    wt_ref,
    bfreq_ref,
    dil_ref,
    wtime_ref,
    btime_ref,
    mix_ref,
    gain_in,
    up_in,
    bup_in,
    down_ref,
    bdown_in,
    lens_ref,
    mean_ref,
    power_ref,
    ends_ref,
    plow_ref,
    phigh_ref,
    low_ref,
    high_ref,
    cor_ref,
    spec_ref,
    send_ref,
    data_ref,
    kron_ref,
    mixed_ref,
    part_ref,
    got_ref,
    up_ref,
    bup_ref,
    bdown_ref,
    gain_ref,
    member_ref,
    frame_sem,
    bin_sem,
    corner_sem,
    chunk_send,
    chunk_recv,
    local_sem,
    sum_send,
    sum_recv,
):
    me = lax.axis_index("band")
    tm = lax.axis_index("tm")
    channels = wt_ref.shape[2]
    groups = channels // SUB
    frames = own_ref.shape[1]
    rows = bins * SUB
    size = kron_ref.shape[0]

    def around(value, count):
        return lax.rem(value + count, count)

    up_tm, down_tm = around(tm + 1, blocks), around(tm - 1, blocks)
    up_band, down_band = around(me + 1, bands), around(me - 1, bands)

    barrier = pltpu.get_barrier_semaphore()

    @pl.loop(1, bands)
    def _(s):
        pl.semaphore_signal(barrier, inc=1, device_id={"band": lax.rem(me + s, bands), "tm": tm}, device_id_type=MESH)

    for t in (up_tm, down_tm):
        for b in (me, up_band, down_band):
            pl.semaphore_signal(barrier, inc=1, device_id={"band": b, "tm": t}, device_id_type=MESH)
    picker = edge_picker(bins)

    @pl.loop(0, groups)
    def _(g):
        at = pl.multiple_of(g * rows, rows)
        small = pl.multiple_of(g * 16, 16)
        edges = jnp.dot(picker, own_ref[pl.ds(at, rows), :], preferred_element_type=jnp.float32)
        plow_ref[pl.ds(small, 16), :] = edges[:16].astype(jnp.bfloat16)
        phigh_ref[pl.ds(small, 16), :] = edges[16:].astype(jnp.bfloat16)

    pl.semaphore_wait(barrier, bands - 1 + 6)

    def remote(src, dst, send, recv, band, block):
        return pltpu.make_async_remote_copy(
            src_ref=src,
            dst_ref=dst,
            send_sem=send,
            recv_sem=recv,
            device_id={"band": band, "tm": block},
            device_id_type=MESH,
        )

    begin, finish = pl.ds(0, 128), pl.ds(frames - 128, 128)
    small_copies = [
        remote(own_ref.at[:, finish], ends_ref.at[0], frame_sem.at[0, 0], frame_sem.at[0, 1], me, up_tm),
        remote(own_ref.at[:, begin], ends_ref.at[1], frame_sem.at[1, 0], frame_sem.at[1, 1], me, down_tm),
    ]
    k = 0
    for i, (lanes, block) in enumerate(((finish, up_tm), (begin, down_tm))):
        for h, (pack, band) in enumerate(((phigh_ref, up_band), (plow_ref, down_band))):
            small_copies.append(
                remote(pack.at[:, lanes], cor_ref.at[i, h], corner_sem.at[k, 0], corner_sem.at[k, 1], band, block)
            )
            k += 1

    def bin_copies(g):
        span = pl.ds(pl.multiple_of(g * 16, 16), 16)
        return (
            remote(phigh_ref.at[span, :], low_ref.at[span, :], bin_sem.at[g, 0, 0], bin_sem.at[g, 0, 1], up_band, tm),
            remote(plow_ref.at[span, :], high_ref.at[span, :], bin_sem.at[g, 1, 0], bin_sem.at[g, 1, 1], down_band, tm),
        )

    for copy in small_copies:
        copy.start()

    @pl.loop(0, groups)
    def _(g):
        for copy in bin_copies(g):
            copy.start()

    def chunk_out(g, s):
        there = lax.rem(me + s, bands)
        place = pl.ds(pl.multiple_of(me * rows, rows), rows)
        return remote(send_ref.at[g, there], data_ref.at[g, place, :], chunk_send.at[g, s], chunk_recv.at[g, s], there, tm)

    def chunk_in(g, s):
        there = lax.rem(me + bands - s, bands)
        place = pl.ds(pl.multiple_of(there * rows, rows), rows)
        return remote(send_ref.at[g, there], data_ref.at[g, place, :], chunk_send.at[g, s], chunk_recv.at[g, s], there, tm)

    def chunk_here(g):
        place = pl.ds(pl.multiple_of(me * rows, rows), rows)
        return pltpu.make_async_copy(send_ref.at[g, me], data_ref.at[g, place, :], local_sem.at[g])

    before_on = jnp.where(tm > 0, 1.0, 0.0).astype(jnp.float32)
    after_on = jnp.where(tm < blocks - 1, 1.0, 0.0).astype(jnp.float32)
    rows_of = (
        wtime_ref[0:1],
        wtime_ref[1:2],
        wtime_ref[2:3],
        btime_ref[...],
        bfreq_ref[...],
        dil_ref[...].astype(jnp.float32),
    )
    for copy in small_copies:
        copy.wait_recv()

    @pl.loop(0, groups)
    def _(g):
        weights = group_weights(wt_ref, g, bins, me > 0, me < bands - 1)
        for copy in bin_copies(g):
            copy.wait_recv()
        front_group(g, bands, weights, own_ref, ends_ref, low_ref, high_ref, cor_ref, rows_of, before_on, after_on, spec_ref, send_ref)

        @pl.loop(1, bands)
        def _(s):
            chunk_out(g, s).start()

        chunk_here(g).start()

    build_kron(mix_ref, kron_ref)
    up_ref[...] = up_in[...].astype(jnp.float32).T.astype(jnp.bfloat16)
    bup_ref[...] = wide(column(bup_in[...], 0, bup_ref.shape[0]))
    bdown_ref[...] = wide(column(bdown_in[...], 0, channels))
    gain_ref[...] = wide(column(gain_in[...], 0, channels))
    lens = lens_ref[...].astype(jnp.float32)
    epochs = lens.shape[1]
    eye_r = lax.broadcasted_iota(jnp.int32, (epochs, epochs), 0)
    eye_c = lax.broadcasted_iota(jnp.int32, (epochs, epochs), 1)
    all_lens = jnp.broadcast_to(lens, (epochs, epochs))
    own_len = jnp.sum(jnp.where(eye_r == eye_c, all_lens, 0.0), axis=1, keepdims=True)
    starts = jnp.sum(jnp.where(eye_c < eye_r, all_lens, 0.0), axis=1, keepdims=True)
    ids = (me * 128 + lax.broadcasted_iota(jnp.int32, (epochs, 128), 1)).astype(jnp.float32)
    member = jnp.where((ids >= starts) & (ids < starts + own_len), 1.0, 0.0)
    member_ref[...] = jnp.concatenate([member, member], axis=1).astype(jnp.bfloat16)

    @pl.loop(0, groups // 2)
    def _(p):
        for g in (2 * p, 2 * p + 1):
            chunk_here(g).wait()

            @pl.loop(1, bands)
            def _(s):
                chunk_in(g, s).wait_recv()

        cols = pl.ds(pl.multiple_of(p * 256, 256), 256)
        both = jnp.concatenate([data_ref[2 * p], data_ref[2 * p + 1]], axis=1)
        step = 256
        for i in range(size // step):
            mixed_ref[i * step : (i + 1) * step, cols] = jnp.dot(
                kron_ref[i * step : (i + 1) * step, :], both, preferred_element_type=jnp.float32
            )

    def sum_out(s):
        there = lax.rem(me + s, bands)
        return remote(part_ref.at[there], got_ref.at[me], sum_send.at[s], sum_recv.at[s], there, tm)

    def sum_in(s):
        there = lax.rem(me + bands - s, bands)
        return remote(part_ref.at[there], got_ref.at[there], sum_send.at[s], sum_recv.at[s], there, tm)

    @pl.loop(1, bands + 1)
    def _(s):
        there = lax.rem(me + s, bands)
        for half in range(bins // some):
            results = back_chunk(
                there * (bins // some) + half, some, groups, data_ref, mixed_ref, up_ref, bup_ref, down_ref, bdown_ref, gain_ref, member_ref
            )
            for k in range(2):
                part_ref[there, k, :, half * some * channels : (half + 1) * some * channels] = results[k]

        @pl.when(s < bands)
        def _():
            sum_out(s).start()

    mean_ref[...] = part_ref[me, 0]
    power_ref[...] = part_ref[me, 1]

    @pl.loop(1, bands)
    def _(s):
        sum_in(s).wait_recv()
        there = lax.rem(me + bands - s, bands)
        mean_ref[...] += got_ref[there, 0]
        power_ref[...] += got_ref[there, 1]

    mean_ref[...] = mean_ref[...] / own_len
    power_ref[...] = power_ref[...] / own_len

    for copy in small_copies:
        copy.wait_send()

    @pl.loop(0, groups)
    def _(g):
        for copy in bin_copies(g):
            copy.wait_send()

        @pl.loop(1, bands)
        def _(s):
            chunk_out(g, s).wait_send()

    @pl.loop(1, bands)
    def _(s):
        sum_out(s).wait_send()


def on_device(
    spectrum,
    w_freq,
    b_freq,
    dilation,
    w_time,
    b_time,
    w_mix,
    ln_gain,
    w_up,
    b_up,
    w_down,
    b_down,
    epoch_lengths,
):
    channels, bins, frames = spectrum.shape
    groups = channels // SUB
    bands = lax.axis_size("band")
    blocks = lax.axis_size("tm")
    hidden = w_up.shape[1]
    epochs = epoch_lengths.shape[1]
    size = bins * bands * SUB
    some = bins // 2
    bf, f32 = jnp.bfloat16, jnp.float32
    vmem = pltpu.VMEM
    dma = pltpu.SemaphoreType.DMA
    return pl.pallas_call(
        functools.partial(kernel, bands, blocks, bins, some),
        out_shape=[jax.ShapeDtypeStruct((epochs, bins * channels), f32)] * 2,
        in_specs=[pl.BlockSpec(memory_space=vmem)] * 13,
        out_specs=[pl.BlockSpec(memory_space=vmem)] * 2,
        scratch_shapes=[
            vmem((2, channels * bins, 128), bf),
            vmem((channels * 2, frames), bf),
            vmem((channels * 2, frames), bf),
            vmem((channels * 2, frames), bf),
            vmem((channels * 2, frames), bf),
            vmem((2, 2, channels * 2, 128), bf),
            vmem((bins * SUB, frames + 2 * REACH), f32),
            vmem((groups, bands, bins * SUB, 128), bf),
            vmem((groups, size, 128), bf),
            vmem((size, size), bf),
            vmem((size, groups * 128), f32),
            vmem((bands, 2, epochs, bins * channels), f32),
            vmem((bands, 2, epochs, bins * channels), f32),
            vmem((hidden, channels), bf),
            vmem((hidden, 128), f32),
            vmem((channels, 128), f32),
            vmem((channels, 128), f32),
            vmem((epochs, 256), bf),
            dma((2, 2)),
            dma((groups, 2, 2)),
            dma((4, 2)),
            dma((groups, bands)),
            dma((groups, bands)),
            dma((groups,)),
            dma((bands,)),
            dma((bands,)),
        ],
        compiler_params=pltpu.CompilerParams(collective_id=0, has_side_effects=True),
        name="whole",
    )(
        spectrum.reshape(channels * bins, frames),
        jnp.transpose(w_freq, (0, 2, 1)),
        b_freq[None],
        dilation[None],
        w_time,
        b_time[None],
        w_mix,
        ln_gain[None],
        w_up,
        b_up[None],
        w_down.T,
        b_down[None],
        epoch_lengths,
    )


def solution(mesh):
    return jax.shard_map(
        on_device,
        mesh=mesh,
        in_specs=(
            P(None, "band", "tm"),
            P(),
            P(),
            P(),
            P(),
            P(),
            P(),
            P(),
            P(),
            P(),
            P(),
            P(),
            P("tm", None),
        ),
        out_specs=(P("tm", "band"), P("tm", "band")),
        check_vma=False,
    )
```

```python
import functools

import jax
import jax.numpy as jnp
from jax import lax
from jax.experimental import pallas as pl
from jax.experimental.pallas import tpu as pltpu
from jax.sharding import PartitionSpec as P

MESH = pl.DeviceIdType.MESH
REACH = 128
SUB = 8
GELU_C = 0.7978845608028654
GELU_A = 0.044715


def gelu_of_half(h):
    inner = h * (2 * GELU_C + (8 * GELU_C * GELU_A) * (h * h))
    return h + h * jnp.tanh(inner)


def three_parts(value):
    first = value.astype(jnp.bfloat16).astype(jnp.float32)
    second = (value - first).astype(jnp.bfloat16).astype(jnp.float32)
    third = (value - first - second).astype(jnp.bfloat16).astype(jnp.float32)
    return first, second, third


def build_kron(mix_ref, kron_ref):
    size = kron_ref.shape[0]
    bins = size // SUB
    one = (
        lax.broadcasted_iota(jnp.int32, (size, bins), 0) // SUB
        == lax.broadcasted_iota(jnp.int32, (size, bins), 1)
    ).astype(jnp.bfloat16)
    tall = jnp.dot(one, mix_ref[...], preferred_element_type=jnp.float32).astype(jnp.bfloat16)
    wide = (
        lax.broadcasted_iota(jnp.int32, (bins, size), 1) // SUB
        == lax.broadcasted_iota(jnp.int32, (bins, size), 0)
    ).astype(jnp.bfloat16)
    kron_ref[...] = jnp.zeros_like(kron_ref)
    step = 256
    rows = lax.broadcasted_iota(jnp.int32, (step, step), 0)
    cols = lax.broadcasted_iota(jnp.int32, (step, step), 1)
    same = (rows % SUB) == (cols % SUB)
    for i in range(size // step):
        for j in range(size // step):
            part = jnp.dot(
                tall[i * step : (i + 1) * step],
                wide[:, j * step : (j + 1) * step],
                preferred_element_type=jnp.float32,
            )
            kron_ref[i * step : (i + 1) * step, j * step : (j + 1) * step] = jnp.where(
                same, part, 0.0
            ).astype(jnp.bfloat16)


def stacked3(tile, groups, row):
    return jnp.concatenate([tile[g, row * SUB : (row + 1) * SUB, :] for g in range(groups)], axis=0)


def stacked(tile, groups, row):
    return jnp.concatenate(
        [tile[row * SUB : (row + 1) * SUB, g * 128 : (g + 1) * 128] for g in range(groups)], axis=0
    )


def raise_chunk(chunk, half, some, groups, mixed_ref, up_ref, gain_ref, act_ref):
    channels = groups * SUB
    rows = some * SUB
    base = pl.multiple_of(chunk * rows, rows)
    mixed = mixed_ref[pl.ds(base, rows), :]
    normed = []
    for r in range(some):
        m = stacked(mixed, groups, r)
        dev = m - jnp.sum(m, axis=0, keepdims=True) * (1.0 / channels)
        var = jnp.sum(dev * dev, axis=0, keepdims=True) * (1.0 / channels)
        normed.append((dev * lax.rsqrt(var + 1e-05) * gain_ref[...]).astype(jnp.bfloat16))
    flat = jnp.concatenate(normed, axis=1)
    flat = jnp.concatenate([flat, jnp.ones((16, some * 128), jnp.bfloat16)], axis=0)
    hidden = jnp.dot(up_ref[...], flat, preferred_element_type=jnp.float32)
    for r in range(some):
        cols = slice(r * 128, (r + 1) * 128)
        act_ref[half, :, cols] = gelu_of_half(hidden[:, cols]).astype(jnp.bfloat16)


def lower_chunk(chunk, act, some, groups, data_ref, down_ref, bdown_ref, member_ref):
    rows = some * SUB
    base = pl.multiple_of(chunk * rows, rows)
    proj = jnp.dot(down_ref[...], act, preferred_element_type=jnp.float32)
    data = data_ref[:, pl.ds(base, rows), :].astype(jnp.float32)
    plain, square = [], []
    for r in range(some):
        block = proj[:, r * 128 : (r + 1) * 128] + bdown_ref[...] + stacked3(data, groups, r)
        for value, store in ((block, plain), (block * block, square)):
            head = value.astype(jnp.bfloat16)
            tail = (value - head.astype(jnp.float32)).astype(jnp.bfloat16)
            store.append(jnp.concatenate([head, tail], axis=1))
    return [
        lax.dot_general(
            member_ref[...],
            jnp.concatenate(store, axis=0),
            (((1,), (1,)), ((), ())),
            preferred_element_type=jnp.float32,
        )
        for store in (plain, square)
    ]


def column(row, first, count):
    lane = lax.broadcasted_iota(jnp.int32, (count, row.shape[1]), 1)
    sub = lax.broadcasted_iota(jnp.int32, (count, row.shape[1]), 0)
    picked = jnp.where(lane == sub + first, jnp.broadcast_to(row, lane.shape), 0.0)
    return jnp.sum(picked, axis=1, keepdims=True)


def wide(col):
    return jnp.broadcast_to(col, (col.shape[0], 128))


def edge_picker(bins):
    shape = (4 * SUB, SUB * bins)
    row = lax.broadcasted_iota(jnp.int32, shape, 0)
    col = lax.broadcasted_iota(jnp.int32, shape, 1)
    edge = row % 2 + jnp.where(row >= 2 * SUB, bins - 2, 0)
    channel = (row % (2 * SUB)) // 2
    return (col == channel * bins + edge).astype(jnp.bfloat16)


def weight_indices(apart_ref, place_ref, order_ref, size, bins, taps, low_on, high_on):
    long = bins + taps - 1
    row = lax.broadcasted_iota(jnp.int32, apart_ref.shape, 0)
    q = lax.broadcasted_iota(jnp.int32, apart_ref.shape, 1)
    apart_ref[...] = jnp.where(q < size * long, row - q // long, -4096)
    place_ref[...] = lax.broadcasted_iota(jnp.int32, place_ref.shape, 1) % long
    p = lax.broadcasted_iota(jnp.int32, order_ref.shape, 1)
    src = lax.broadcasted_iota(jnp.int32, order_ref.shape, 0)
    inner = size * bins
    lo = p - inner
    hi = lo - 2 * size
    wanted = jnp.where(
        p < inner,
        (p // bins) * long + p % bins + 2,
        jnp.where(
            lo < 2 * size,
            (lo // 2) * long + lo % 2 + jnp.where(low_on, 0, 4096),
            (hi // 2) * long + bins + 2 + hi % 2 + jnp.where(high_on, 0, 4096),
        ),
    )
    order_ref[...] = ((src == wanted) & (p < size * long)).astype(jnp.bfloat16)


def group_weights(wt_ref, g, bins, apart_ref, place_ref, order_ref):
    taps, size, channels = wt_ref.shape
    wid = size * (bins + taps - 1)
    pick = (apart_ref[...] == g * size).astype(jnp.bfloat16)
    place = place_ref[...]
    base = jnp.zeros((size, 128), jnp.float32)
    for k in range(taps):
        spread = jnp.dot(wt_ref[k], pick, preferred_element_type=jnp.float32)
        base = jnp.where(place == k, spread, base)
    base = 0.5 * base
    turned = [base] + [pltpu.roll(base, f, 1) for f in range(1, bins)]
    big = jnp.concatenate(turned, axis=0).astype(jnp.bfloat16)
    ready = jnp.dot(big, order_ref[...], preferred_element_type=jnp.float32)
    return ready[:, :wid].astype(jnp.bfloat16)


def front_group(g, bands, weights, own_ref, ends_ref, low_ref, high_ref, cor_ref, rows_of, before_on, after_on, spec_ref, send_ref):
    rows = weights.shape[0]
    long = own_ref.shape[1]
    t0, t1, t2, shift, bias8, step = (wide(column(r, g * SUB, SUB)) for r in rows_of)
    bias = jnp.concatenate([0.5 * bias8] * (rows // SUB), axis=0)
    tiles = long // 128 + 2
    at = pl.multiple_of(g * rows, rows)
    small = pl.multiple_of(g * 16, 16)
    body = jnp.concatenate(
        [own_ref[pl.ds(at, rows), :], low_ref[pl.ds(small, 16), :], high_ref[pl.ds(small, 16), :]],
        axis=0,
    )
    first, last = (
        jnp.concatenate(
            [
                ends_ref[i, pl.ds(at, rows), :],
                cor_ref[i, 0, pl.ds(small, 16), :],
                cor_ref[i, 1, pl.ds(small, 16), :],
            ],
            axis=0,
        )
        for i in range(2)
    )
    data = jnp.concatenate([first, body, last], axis=1)
    pre = jnp.dot(weights, data, preferred_element_type=jnp.float32)
    step = step.astype(jnp.int32)
    for j in range(tiles):
        cols = slice(j * 128, (j + 1) * 128)
        act = gelu_of_half(pre[:, cols] + bias)
        if j == 0:
            act = act * before_on
        if j == tiles - 1:
            act = act * after_on
        spec_ref[:, cols] = act.astype(jnp.bfloat16).astype(jnp.float32)
    lane = lax.broadcasted_iota(jnp.int32, (SUB, 128), 1)
    from_left = (lane - step) & 127
    from_right = (lane + step) & 127
    keep_left = lane >= step
    keep_right = lane + step < 128

    def take(value, index):
        return jnp.take_along_axis(value, index, axis=1, mode="promise_in_bounds")

    def half(start):
        v = [spec_ref[start : start + SUB, j * 128 : (j + 1) * 128] for j in range(tiles)]
        left = [take(v[j], from_left) for j in range(tiles - 1)]
        right = [take(v[j], from_right) for j in range(1, tiles)]
        outs = []
        for j in range(1, tiles - 1):
            a = jnp.where(keep_left, left[j], left[j - 1])
            c = jnp.where(keep_right, right[j - 1], right[j])
            outs.append(t0 * a + t1 * v[j] + t2 * c + shift)
        return outs

    for pair in range(rows // 16):
        top = half(pair * 16)
        bottom = half(pair * 16 + SUB)
        for j in range(bands):
            both = jnp.concatenate([top[j], bottom[j]], axis=0)
            send_ref[g, j, pair * 16 : (pair + 1) * 16, :] = both.astype(jnp.bfloat16)


def kernel(
    bands,
    blocks,
    bins,
    some,
    own_ref,
    wt_ref,
    bfreq_ref,
    dil_ref,
    wtime_ref,
    btime_ref,
    mix_ref,
    gain_in,
    up_in,
    bup_in,
    down_ref,
    bdown_in,
    lens_ref,
    out_ref,
    ends_ref,
    plow_ref,
    phigh_ref,
    low_ref,
    high_ref,
    cor_ref,
    spec_ref,
    send_ref,
    data_ref,
    kron_ref,
    mixed_ref,
    part_ref,
    got_ref,
    up_ref,
    bdown_ref,
    gain_ref,
    member_ref,
    apart_ref,
    place_ref,
    order_ref,
    wall_ref,
    act_ref,
    frame_sem,
    bin_sem,
    corner_sem,
    chunk_send,
    chunk_recv,
    local_sem,
    sum_send,
    sum_recv,
):
    me = lax.axis_index("band")
    tm = lax.axis_index("tm")
    channels = wt_ref.shape[2]
    groups = channels // SUB
    frames = own_ref.shape[1]
    rows = bins * SUB
    size = kron_ref.shape[0]

    def around(value, count):
        return lax.rem(value + count, count)

    up_tm, down_tm = around(tm + 1, blocks), around(tm - 1, blocks)
    up_band, down_band = around(me + 1, bands), around(me - 1, bands)

    barrier = pltpu.get_barrier_semaphore()

    @pl.loop(1, bands)
    def _(s):
        pl.semaphore_signal(barrier, inc=1, device_id={"band": lax.rem(me + s, bands), "tm": tm}, device_id_type=MESH)

    for t in (up_tm, down_tm):
        for b in (me, up_band, down_band):
            pl.semaphore_signal(barrier, inc=1, device_id={"band": b, "tm": t}, device_id_type=MESH)
    picker = edge_picker(bins)

    @pl.loop(0, groups)
    def _(g):
        at = pl.multiple_of(g * rows, rows)
        small = pl.multiple_of(g * 16, 16)
        edges = jnp.dot(picker, own_ref[pl.ds(at, rows), :], preferred_element_type=jnp.float32)
        plow_ref[pl.ds(small, 16), :] = edges[:16].astype(jnp.bfloat16)
        phigh_ref[pl.ds(small, 16), :] = edges[16:].astype(jnp.bfloat16)

    pl.semaphore_wait(barrier, bands - 1 + 6)

    def remote(src, dst, send, recv, band, block):
        return pltpu.make_async_remote_copy(
            src_ref=src,
            dst_ref=dst,
            send_sem=send,
            recv_sem=recv,
            device_id={"band": band, "tm": block},
            device_id_type=MESH,
        )

    begin, finish = pl.ds(0, 128), pl.ds(frames - 128, 128)
    small_copies = [
        remote(own_ref.at[:, finish], ends_ref.at[0], frame_sem.at[0, 0], frame_sem.at[0, 1], me, up_tm),
        remote(own_ref.at[:, begin], ends_ref.at[1], frame_sem.at[1, 0], frame_sem.at[1, 1], me, down_tm),
    ]
    k = 0
    for i, (lanes, block) in enumerate(((finish, up_tm), (begin, down_tm))):
        for h, (pack, band) in enumerate(((phigh_ref, up_band), (plow_ref, down_band))):
            small_copies.append(
                remote(pack.at[:, lanes], cor_ref.at[i, h], corner_sem.at[k, 0], corner_sem.at[k, 1], band, block)
            )
            k += 1

    def bin_copies(g):
        span = pl.ds(pl.multiple_of(g * 16, 16), 16)
        return (
            remote(phigh_ref.at[span, :], low_ref.at[span, :], bin_sem.at[g, 0, 0], bin_sem.at[g, 0, 1], up_band, tm),
            remote(plow_ref.at[span, :], high_ref.at[span, :], bin_sem.at[g, 1, 0], bin_sem.at[g, 1, 1], down_band, tm),
        )

    for copy in small_copies:
        copy.start()

    @pl.loop(0, groups)
    def _(g):
        for copy in bin_copies(g):
            copy.start()

    def chunk_out(g, s):
        there = lax.rem(me + s, bands)
        place = pl.ds(pl.multiple_of(me * rows, rows), rows)
        return remote(send_ref.at[g, there], data_ref.at[g, place, :], chunk_send.at[g, s], chunk_recv.at[g, s], there, tm)

    def chunk_in(g, s):
        there = lax.rem(me + bands - s, bands)
        place = pl.ds(pl.multiple_of(there * rows, rows), rows)
        return remote(send_ref.at[g, there], data_ref.at[g, place, :], chunk_send.at[g, s], chunk_recv.at[g, s], there, tm)

    def chunk_here(g):
        place = pl.ds(pl.multiple_of(me * rows, rows), rows)
        return pltpu.make_async_copy(send_ref.at[g, me], data_ref.at[g, place, :], local_sem.at[g])

    before_on = jnp.where(tm > 0, 1.0, 0.0).astype(jnp.float32)
    after_on = jnp.where(tm < blocks - 1, 1.0, 0.0).astype(jnp.float32)
    rows_of = (
        wtime_ref[0:1],
        wtime_ref[1:2],
        wtime_ref[2:3],
        btime_ref[...],
        bfreq_ref[...],
        dil_ref[...].astype(jnp.float32),
    )
    weight_indices(apart_ref, place_ref, order_ref, SUB, bins, wt_ref.shape[0], me > 0, me < bands - 1)

    @pl.loop(0, groups)
    def _(g):
        wall_ref[g] = group_weights(wt_ref, g, bins, apart_ref, place_ref, order_ref)

    sub = lax.broadcasted_iota(jnp.int32, (16, up_in.shape[1]), 0)
    extra = jnp.zeros(sub.shape, jnp.float32)
    for i, piece in enumerate(three_parts(bup_in[...])):
        extra = jnp.where(sub == i, piece, extra)
    tall = 0.5 * jnp.concatenate([up_in[...].astype(jnp.float32), extra], axis=0)
    up_ref[...] = tall.T.astype(jnp.bfloat16)
    bdown_ref[...] = wide(column(bdown_in[...], 0, channels))
    gain_ref[...] = wide(column(gain_in[...], 0, channels))
    lens = lens_ref[...].astype(jnp.float32)
    epochs = lens.shape[1]
    eye_r = lax.broadcasted_iota(jnp.int32, (epochs, epochs), 0)
    eye_c = lax.broadcasted_iota(jnp.int32, (epochs, epochs), 1)
    all_lens = jnp.broadcast_to(lens, (epochs, epochs))
    own_len = jnp.sum(jnp.where(eye_r == eye_c, all_lens, 0.0), axis=1, keepdims=True)
    starts = jnp.sum(jnp.where(eye_c < eye_r, all_lens, 0.0), axis=1, keepdims=True)
    ids = (me * 128 + lax.broadcasted_iota(jnp.int32, (epochs, 128), 1)).astype(jnp.float32)
    member = jnp.where((ids >= starts) & (ids < starts + own_len), 1.0, 0.0)
    member_ref[...] = jnp.concatenate([member, member], axis=1).astype(jnp.bfloat16)

    for copy in small_copies:
        copy.wait_recv()

    @pl.loop(0, groups)
    def _(g):
        for copy in bin_copies(g):
            copy.wait_recv()
        front_group(g, bands, wall_ref[g], own_ref, ends_ref, low_ref, high_ref, cor_ref, rows_of, before_on, after_on, spec_ref, send_ref)

        @pl.loop(1, bands)
        def _(s):
            chunk_out(g, s).start()

        chunk_here(g).start()

    build_kron(mix_ref, kron_ref)

    @pl.loop(0, groups // 2)
    def _(p):
        for g in (2 * p, 2 * p + 1):
            chunk_here(g).wait()

            @pl.loop(1, bands)
            def _(s):
                chunk_in(g, s).wait_recv()

        cols = pl.ds(pl.multiple_of(p * 256, 256), 256)
        both = jnp.concatenate([data_ref[2 * p], data_ref[2 * p + 1]], axis=1)
        step = 256
        for i in range(size // step):
            mixed_ref[i * step : (i + 1) * step, cols] = jnp.dot(
                kron_ref[i * step : (i + 1) * step, :], both, preferred_element_type=jnp.float32
            )

    def sum_out(s):
        there = lax.rem(me + s, bands)
        return remote(part_ref.at[there], got_ref.at[me], sum_send.at[s], sum_recv.at[s], there, tm)

    def sum_in(s):
        there = lax.rem(me + bands - s, bands)
        return remote(part_ref.at[there], got_ref.at[there], sum_send.at[s], sum_recv.at[s], there, tm)

    halves = bins // some

    def raise_bins(s):
        there = lax.rem(me + s, bands)
        for half in range(halves):
            raise_chunk(there * halves + half, half, some, groups, mixed_ref, up_ref, gain_ref, act_ref)

    def lower_bins(s, acts):
        there = lax.rem(me + s, bands)
        for half in range(halves):
            results = lower_chunk(there * halves + half, acts[half], some, groups, data_ref, down_ref, bdown_ref, member_ref)
            for k in range(2):
                part_ref[there, k, :, half * some * channels : (half + 1) * some * channels] = results[k]

    raise_bins(1)

    @pl.loop(1, bands)
    def _(s):
        acts = [act_ref[half] for half in range(halves)]
        lower_bins(s, acts)
        raise_bins(s + 1)
        sum_out(s).start()

    lower_bins(bands, [act_ref[half] for half in range(halves)])

    out_ref[...] = part_ref[me]

    @pl.loop(1, bands)
    def _(s):
        sum_in(s).wait_recv()
        there = lax.rem(me + bands - s, bands)
        out_ref[...] += got_ref[there]

    for copy in small_copies:
        copy.wait_send()

    @pl.loop(0, groups)
    def _(g):
        for copy in bin_copies(g):
            copy.wait_send()

        @pl.loop(1, bands)
        def _(s):
            chunk_out(g, s).wait_send()

    @pl.loop(1, bands)
    def _(s):
        sum_out(s).wait_send()


def on_device(
    spectrum,
    w_freq,
    b_freq,
    dilation,
    w_time,
    b_time,
    w_mix,
    ln_gain,
    w_up,
    b_up,
    w_down,
    b_down,
    epoch_lengths,
):
    channels, bins, frames = spectrum.shape
    groups = channels // SUB
    bands = lax.axis_size("band")
    blocks = lax.axis_size("tm")
    hidden = w_up.shape[1]
    epochs = epoch_lengths.shape[1]
    size = bins * bands * SUB
    some = bins // 2
    bf, f32 = jnp.bfloat16, jnp.float32
    vmem = pltpu.VMEM
    dma = pltpu.SemaphoreType.DMA
    totals = pl.pallas_call(
        functools.partial(kernel, bands, blocks, bins, some),
        out_shape=jax.ShapeDtypeStruct((2, epochs, bins * channels), f32),
        in_specs=[pl.BlockSpec(memory_space=vmem)] * 13,
        out_specs=pl.BlockSpec(memory_space=vmem),
        scratch_shapes=[
            vmem((2, channels * bins, 128), bf),
            vmem((channels * 2, frames), bf),
            vmem((channels * 2, frames), bf),
            vmem((channels * 2, frames), bf),
            vmem((channels * 2, frames), bf),
            vmem((2, 2, channels * 2, 128), bf),
            vmem((bins * SUB, frames + 2 * REACH), f32),
            vmem((groups, bands, bins * SUB, 128), bf),
            vmem((groups, size, 128), bf),
            vmem((size, size), bf),
            vmem((size, groups * 128), f32),
            vmem((bands, 2, epochs, bins * channels), f32),
            vmem((bands, 2, epochs, bins * channels), f32),
            vmem((hidden, channels + 16), bf),
            vmem((channels, 128), f32),
            vmem((channels, 128), f32),
            vmem((epochs, 256), bf),
            vmem((channels, 128), jnp.int32),
            vmem((SUB, 128), jnp.int32),
            vmem((128, 128), bf),
            vmem((groups, bins * SUB, SUB * (bins + 4)), bf),
            vmem((2, hidden, some * 128), bf),
            dma((2, 2)),
            dma((groups, 2, 2)),
            dma((4, 2)),
            dma((groups, bands)),
            dma((groups, bands)),
            dma((groups,)),
            dma((bands,)),
            dma((bands,)),
        ],
        compiler_params=pltpu.CompilerParams(collective_id=0, has_side_effects=True),
        name="whole",
    )(
        spectrum.reshape(channels * bins, frames),
        jnp.transpose(w_freq, (0, 2, 1)),
        b_freq[None],
        dilation[None],
        w_time,
        b_time[None],
        w_mix,
        ln_gain[None],
        w_up,
        b_up[None],
        w_down.T,
        b_down[None],
        epoch_lengths,
    )
    lens = epoch_lengths[0].astype(f32)[:, None]
    return totals[0] / lens, totals[1] / lens


def solution(mesh):
    return jax.shard_map(
        on_device,
        mesh=mesh,
        in_specs=(
            P(None, "band", "tm"),
            P(),
            P(),
            P(),
            P(),
            P(),
            P(),
            P(),
            P(),
            P(),
            P(),
            P(),
            P("tm", None),
        ),
        out_specs=(P("tm", "band"), P("tm", "band")),
        check_vma=False,
    )
```

```python
import functools

import jax
import jax.numpy as jnp
from jax import lax
from jax.experimental import pallas as pl
from jax.experimental.pallas import tpu as pltpu
from jax.sharding import PartitionSpec as P

MESH = pl.DeviceIdType.MESH
REACH = 128
SUB = 8
GELU_C = 0.7978845608028654
GELU_A = 0.044715


def gelu_of_half(h):
    inner = h * (2 * GELU_C + (8 * GELU_C * GELU_A) * (h * h))
    return h + h * jnp.tanh(inner)


def gelu_of_half_narrow(h):
    inner = h * (jnp.bfloat16(2 * GELU_C) + jnp.bfloat16(8 * GELU_C * GELU_A) * (h * h))
    return h + h * jnp.tanh(inner)


def three_parts(value):
    first = value.astype(jnp.bfloat16).astype(jnp.float32)
    second = (value - first).astype(jnp.bfloat16).astype(jnp.float32)
    third = (value - first - second).astype(jnp.bfloat16).astype(jnp.float32)
    return first, second, third


def build_kron(mix_ref, kron_ref):
    size = kron_ref.shape[0]
    bins = size // SUB
    one = (
        lax.broadcasted_iota(jnp.int32, (size, bins), 0) // SUB
        == lax.broadcasted_iota(jnp.int32, (size, bins), 1)
    ).astype(jnp.bfloat16)
    tall = jnp.dot(one, mix_ref[...], preferred_element_type=jnp.float32).astype(jnp.bfloat16)
    wide = (
        lax.broadcasted_iota(jnp.int32, (bins, size), 1) // SUB
        == lax.broadcasted_iota(jnp.int32, (bins, size), 0)
    ).astype(jnp.bfloat16)
    kron_ref[...] = jnp.zeros_like(kron_ref)
    step = 256
    rows = lax.broadcasted_iota(jnp.int32, (step, step), 0)
    cols = lax.broadcasted_iota(jnp.int32, (step, step), 1)
    same = (rows % SUB) == (cols % SUB)
    for i in range(size // step):
        for j in range(size // step):
            part = jnp.dot(
                tall[i * step : (i + 1) * step],
                wide[:, j * step : (j + 1) * step],
                preferred_element_type=jnp.float32,
            )
            kron_ref[i * step : (i + 1) * step, j * step : (j + 1) * step] = jnp.where(
                same, part, 0.0
            ).astype(jnp.bfloat16)


def stacked3(tile, groups, row):
    return jnp.concatenate([tile[g, row * SUB : (row + 1) * SUB, :] for g in range(groups)], axis=0)


def stacked(tile, groups, row):
    return jnp.concatenate(
        [tile[row * SUB : (row + 1) * SUB, g * 128 : (g + 1) * 128] for g in range(groups)], axis=0
    )


def norm_chunk(chunk, some, groups, mixed_ref, gain_ref):
    channels = groups * SUB
    rows = some * SUB
    base = pl.multiple_of(chunk * rows, rows)
    mixed = mixed_ref[pl.ds(base, rows), :]
    normed = []
    for r in range(some):
        m = stacked(mixed, groups, r)
        dev = m - jnp.sum(m, axis=0, keepdims=True) * (1.0 / channels)
        var = jnp.sum(dev * dev, axis=0, keepdims=True) * (1.0 / channels)
        normed.append((dev * lax.rsqrt(var + 1e-05) * gain_ref[...]).astype(jnp.bfloat16))
    flat = jnp.concatenate(normed, axis=1)
    return jnp.concatenate([flat, jnp.ones((16, some * 128), jnp.bfloat16)], axis=0)


def raise_chunk(flat, half, some, up_ref, act_ref):
    hidden = jnp.dot(up_ref[...], flat, preferred_element_type=jnp.float32)
    for r in range(some):
        cols = slice(r * 128, (r + 1) * 128)
        act_ref[half, :, cols] = gelu_of_half_narrow(hidden[:, cols].astype(jnp.bfloat16))


def lower_chunk(chunk, proj, some, groups, data_ref, bdown_ref, member_ref):
    rows = some * SUB
    base = pl.multiple_of(chunk * rows, rows)
    data = data_ref[:, pl.ds(base, rows), :].astype(jnp.float32)
    plain, square = [], []
    for r in range(some):
        block = proj[:, r * 128 : (r + 1) * 128] + bdown_ref[...] + stacked3(data, groups, r)
        for value, store in ((block, plain), (block * block, square)):
            head = value.astype(jnp.bfloat16)
            tail = (value - head.astype(jnp.float32)).astype(jnp.bfloat16)
            store.append(jnp.concatenate([head, tail], axis=1))
    return [
        lax.dot_general(
            member_ref[...],
            jnp.concatenate(store, axis=0),
            (((1,), (1,)), ((), ())),
            preferred_element_type=jnp.float32,
        )
        for store in (plain, square)
    ]


def column(row, first, count):
    lane = lax.broadcasted_iota(jnp.int32, (count, row.shape[1]), 1)
    sub = lax.broadcasted_iota(jnp.int32, (count, row.shape[1]), 0)
    picked = jnp.where(lane == sub + first, jnp.broadcast_to(row, lane.shape), 0.0)
    return jnp.sum(picked, axis=1, keepdims=True)


def wide(col):
    return jnp.broadcast_to(col, (col.shape[0], 128))


def edge_picker(bins):
    shape = (4 * SUB, SUB * bins)
    row = lax.broadcasted_iota(jnp.int32, shape, 0)
    col = lax.broadcasted_iota(jnp.int32, shape, 1)
    edge = row % 2 + jnp.where(row >= 2 * SUB, bins - 2, 0)
    channel = (row % (2 * SUB)) // 2
    return (col == channel * bins + edge).astype(jnp.bfloat16)


def weight_indices(apart_ref, place_ref, order_ref, size, bins, taps, low_on, high_on):
    long = bins + taps - 1
    row = lax.broadcasted_iota(jnp.int32, apart_ref.shape, 0)
    q = lax.broadcasted_iota(jnp.int32, apart_ref.shape, 1)
    apart_ref[...] = jnp.where(q < size * long, row - q // long, -4096)
    place_ref[...] = lax.broadcasted_iota(jnp.int32, place_ref.shape, 1) % long
    p = lax.broadcasted_iota(jnp.int32, order_ref.shape, 1)
    src = lax.broadcasted_iota(jnp.int32, order_ref.shape, 0)
    inner = size * bins
    lo = p - inner
    hi = lo - 2 * size
    wanted = jnp.where(
        p < inner,
        (p // bins) * long + p % bins + 2,
        jnp.where(
            lo < 2 * size,
            (lo // 2) * long + lo % 2 + jnp.where(low_on, 0, 4096),
            (hi // 2) * long + bins + 2 + hi % 2 + jnp.where(high_on, 0, 4096),
        ),
    )
    order_ref[...] = ((src == wanted) & (p < size * long)).astype(jnp.bfloat16)


def group_weights(wt_ref, g, bins, apart_ref, place_ref, order_ref):
    taps, size, channels = wt_ref.shape
    wid = size * (bins + taps - 1)
    pick = (apart_ref[...] == g * size).astype(jnp.bfloat16)
    place = place_ref[...]
    base = jnp.zeros((size, 128), jnp.float32)
    for k in range(taps):
        spread = jnp.dot(wt_ref[k], pick, preferred_element_type=jnp.float32)
        base = jnp.where(place == k, spread, base)
    base = 0.5 * base
    turned = [base] + [pltpu.roll(base, f, 1) for f in range(1, bins)]
    big = jnp.concatenate(turned, axis=0).astype(jnp.bfloat16)
    ready = jnp.dot(big, order_ref[...], preferred_element_type=jnp.float32)
    return ready[:, :wid].astype(jnp.bfloat16)


def front_group(g, bands, weights, own_ref, ends_ref, low_ref, high_ref, cor_ref, rows_of, before_on, after_on, spec_ref, send_ref):
    rows = weights.shape[0]
    long = own_ref.shape[1]
    t0, t1, t2, shift, bias8, step = (wide(column(r, g * SUB, SUB)) for r in rows_of)
    bias = jnp.concatenate([0.5 * bias8] * (rows // SUB), axis=0)
    tiles = long // 128 + 2
    at = pl.multiple_of(g * rows, rows)
    small = pl.multiple_of(g * 16, 16)
    body = jnp.concatenate(
        [own_ref[pl.ds(at, rows), :], low_ref[pl.ds(small, 16), :], high_ref[pl.ds(small, 16), :]],
        axis=0,
    )
    first, last = (
        jnp.concatenate(
            [
                ends_ref[i, pl.ds(at, rows), :],
                cor_ref[i, 0, pl.ds(small, 16), :],
                cor_ref[i, 1, pl.ds(small, 16), :],
            ],
            axis=0,
        )
        for i in range(2)
    )
    data = jnp.concatenate([first, body, last], axis=1)
    pre = jnp.dot(weights, data, preferred_element_type=jnp.float32)
    step = step.astype(jnp.int32)
    for j in range(tiles):
        cols = slice(j * 128, (j + 1) * 128)
        act = gelu_of_half(pre[:, cols] + bias)
        if j == 0:
            act = act * before_on
        if j == tiles - 1:
            act = act * after_on
        spec_ref[:, cols] = act.astype(jnp.bfloat16).astype(jnp.float32)
    lane = lax.broadcasted_iota(jnp.int32, (SUB, 128), 1)
    from_left = (lane - step) & 127
    from_right = (lane + step) & 127
    keep_left = lane >= step
    keep_right = lane + step < 128

    def take(value, index):
        return jnp.take_along_axis(value, index, axis=1, mode="promise_in_bounds")

    def half(start):
        v = [spec_ref[start : start + SUB, j * 128 : (j + 1) * 128] for j in range(tiles)]
        left = [take(v[j], from_left) for j in range(tiles - 1)]
        right = [take(v[j], from_right) for j in range(1, tiles)]
        outs = []
        for j in range(1, tiles - 1):
            a = jnp.where(keep_left, left[j], left[j - 1])
            c = jnp.where(keep_right, right[j - 1], right[j])
            outs.append(t0 * a + t1 * v[j] + t2 * c + shift)
        return outs

    for pair in range(rows // 16):
        top = half(pair * 16)
        bottom = half(pair * 16 + SUB)
        for j in range(bands):
            both = jnp.concatenate([top[j], bottom[j]], axis=0)
            send_ref[g, j, pair * 16 : (pair + 1) * 16, :] = both.astype(jnp.bfloat16)


def kernel(
    bands,
    blocks,
    bins,
    some,
    own_ref,
    wt_ref,
    bfreq_ref,
    dil_ref,
    wtime_ref,
    btime_ref,
    mix_ref,
    gain_in,
    up_in,
    bup_in,
    down_ref,
    bdown_in,
    lens_ref,
    out_ref,
    ends_ref,
    plow_ref,
    phigh_ref,
    low_ref,
    high_ref,
    cor_ref,
    spec_ref,
    send_ref,
    data_ref,
    kron_ref,
    mixed_ref,
    part_ref,
    got_ref,
    up_ref,
    bdown_ref,
    gain_ref,
    member_ref,
    apart_ref,
    place_ref,
    order_ref,
    wall_ref,
    act_ref,
    frame_sem,
    bin_sem,
    corner_sem,
    chunk_send,
    chunk_recv,
    local_sem,
    sum_send,
    sum_recv,
):
    me = lax.axis_index("band")
    tm = lax.axis_index("tm")
    channels = wt_ref.shape[2]
    groups = channels // SUB
    frames = own_ref.shape[1]
    rows = bins * SUB
    size = kron_ref.shape[0]

    def around(value, count):
        return lax.rem(value + count, count)

    up_tm, down_tm = around(tm + 1, blocks), around(tm - 1, blocks)
    up_band, down_band = around(me + 1, bands), around(me - 1, bands)

    barrier = pltpu.get_barrier_semaphore()

    @pl.loop(1, bands)
    def _(s):
        pl.semaphore_signal(barrier, inc=1, device_id={"band": lax.rem(me + s, bands), "tm": tm}, device_id_type=MESH)

    for t in (up_tm, down_tm):
        for b in (me, up_band, down_band):
            pl.semaphore_signal(barrier, inc=1, device_id={"band": b, "tm": t}, device_id_type=MESH)
    picker = edge_picker(bins)

    @pl.loop(0, groups)
    def _(g):
        at = pl.multiple_of(g * rows, rows)
        small = pl.multiple_of(g * 16, 16)
        edges = jnp.dot(picker, own_ref[pl.ds(at, rows), :], preferred_element_type=jnp.float32)
        plow_ref[pl.ds(small, 16), :] = edges[:16].astype(jnp.bfloat16)
        phigh_ref[pl.ds(small, 16), :] = edges[16:].astype(jnp.bfloat16)

    pl.semaphore_wait(barrier, bands - 1 + 6)

    def remote(src, dst, send, recv, band, block):
        return pltpu.make_async_remote_copy(
            src_ref=src,
            dst_ref=dst,
            send_sem=send,
            recv_sem=recv,
            device_id={"band": band, "tm": block},
            device_id_type=MESH,
        )

    begin, finish = pl.ds(0, 128), pl.ds(frames - 128, 128)
    small_copies = [
        remote(own_ref.at[:, finish], ends_ref.at[0], frame_sem.at[0, 0], frame_sem.at[0, 1], me, up_tm),
        remote(own_ref.at[:, begin], ends_ref.at[1], frame_sem.at[1, 0], frame_sem.at[1, 1], me, down_tm),
    ]
    k = 0
    for i, (lanes, block) in enumerate(((finish, up_tm), (begin, down_tm))):
        for h, (pack, band) in enumerate(((phigh_ref, up_band), (plow_ref, down_band))):
            small_copies.append(
                remote(pack.at[:, lanes], cor_ref.at[i, h], corner_sem.at[k, 0], corner_sem.at[k, 1], band, block)
            )
            k += 1

    def bin_copies(g):
        span = pl.ds(pl.multiple_of(g * 16, 16), 16)
        return (
            remote(phigh_ref.at[span, :], low_ref.at[span, :], bin_sem.at[g, 0, 0], bin_sem.at[g, 0, 1], up_band, tm),
            remote(plow_ref.at[span, :], high_ref.at[span, :], bin_sem.at[g, 1, 0], bin_sem.at[g, 1, 1], down_band, tm),
        )

    for copy in small_copies:
        copy.start()

    @pl.loop(0, groups)
    def _(g):
        for copy in bin_copies(g):
            copy.start()

    def chunk_out(g, s):
        there = lax.rem(me + s, bands)
        place = pl.ds(pl.multiple_of(me * rows, rows), rows)
        return remote(send_ref.at[g, there], data_ref.at[g, place, :], chunk_send.at[g, s], chunk_recv.at[g, s], there, tm)

    def chunk_in(g, s):
        there = lax.rem(me + bands - s, bands)
        place = pl.ds(pl.multiple_of(there * rows, rows), rows)
        return remote(send_ref.at[g, there], data_ref.at[g, place, :], chunk_send.at[g, s], chunk_recv.at[g, s], there, tm)

    def chunk_here(g):
        place = pl.ds(pl.multiple_of(me * rows, rows), rows)
        return pltpu.make_async_copy(send_ref.at[g, me], data_ref.at[g, place, :], local_sem.at[g])

    before_on = jnp.where(tm > 0, 1.0, 0.0).astype(jnp.float32)
    after_on = jnp.where(tm < blocks - 1, 1.0, 0.0).astype(jnp.float32)
    rows_of = (
        wtime_ref[0:1],
        wtime_ref[1:2],
        wtime_ref[2:3],
        btime_ref[...],
        bfreq_ref[...],
        dil_ref[...].astype(jnp.float32),
    )
    weight_indices(apart_ref, place_ref, order_ref, SUB, bins, wt_ref.shape[0], me > 0, me < bands - 1)

    @pl.loop(0, groups)
    def _(g):
        wall_ref[g] = group_weights(wt_ref, g, bins, apart_ref, place_ref, order_ref)

    sub = lax.broadcasted_iota(jnp.int32, (16, up_in.shape[1]), 0)
    extra = jnp.zeros(sub.shape, jnp.float32)
    for i, piece in enumerate(three_parts(bup_in[...])):
        extra = jnp.where(sub == i, piece, extra)
    tall = 0.5 * jnp.concatenate([up_in[...].astype(jnp.float32), extra], axis=0)
    up_ref[...] = tall.T.astype(jnp.bfloat16)
    bdown_ref[...] = wide(column(bdown_in[...], 0, channels))
    gain_ref[...] = wide(column(gain_in[...], 0, channels))
    lens = lens_ref[...].astype(jnp.float32)
    epochs = lens.shape[1]
    eye_r = lax.broadcasted_iota(jnp.int32, (epochs, epochs), 0)
    eye_c = lax.broadcasted_iota(jnp.int32, (epochs, epochs), 1)
    all_lens = jnp.broadcast_to(lens, (epochs, epochs))
    own_len = jnp.sum(jnp.where(eye_r == eye_c, all_lens, 0.0), axis=1, keepdims=True)
    starts = jnp.sum(jnp.where(eye_c < eye_r, all_lens, 0.0), axis=1, keepdims=True)
    ids = (me * 128 + lax.broadcasted_iota(jnp.int32, (epochs, 128), 1)).astype(jnp.float32)
    member = jnp.where((ids >= starts) & (ids < starts + own_len), 1.0, 0.0)
    member_ref[...] = jnp.concatenate([member, member], axis=1).astype(jnp.bfloat16)

    for copy in small_copies:
        copy.wait_recv()

    @pl.loop(0, groups)
    def _(g):
        for copy in bin_copies(g):
            copy.wait_recv()
        front_group(g, bands, wall_ref[g], own_ref, ends_ref, low_ref, high_ref, cor_ref, rows_of, before_on, after_on, spec_ref, send_ref)

        @pl.loop(1, bands)
        def _(s):
            chunk_out(g, s).start()

        chunk_here(g).start()

    build_kron(mix_ref, kron_ref)

    @pl.loop(0, groups // 2)
    def _(p):
        for g in (2 * p, 2 * p + 1):
            chunk_here(g).wait()

            @pl.loop(1, bands)
            def _(s):
                chunk_in(g, s).wait_recv()

        cols = pl.ds(pl.multiple_of(p * 256, 256), 256)
        both = jnp.concatenate([data_ref[2 * p], data_ref[2 * p + 1]], axis=1)
        step = 256
        for i in range(size // step):
            mixed_ref[i * step : (i + 1) * step, cols] = jnp.dot(
                kron_ref[i * step : (i + 1) * step, :], both, preferred_element_type=jnp.float32
            )

    def sum_out(s):
        there = lax.rem(me + s, bands)
        return remote(part_ref.at[there], got_ref.at[me], sum_send.at[s], sum_recv.at[s], there, tm)

    def sum_in(s):
        there = lax.rem(me + bands - s, bands)
        return remote(part_ref.at[there], got_ref.at[there], sum_send.at[s], sum_recv.at[s], there, tm)

    halves = bins // some

    def chunk_of(s, half):
        return lax.rem(me + s, bands) * halves + half

    def norms(s):
        return [norm_chunk(chunk_of(s, half), some, groups, mixed_ref, gain_ref) for half in range(halves)]

    def downs():
        return [
            jnp.dot(down_ref[...], act_ref[half], preferred_element_type=jnp.float32)
            for half in range(halves)
        ]

    def lower_half(s, half, proj):
        results = lower_chunk(chunk_of(s, half), proj, some, groups, data_ref, bdown_ref, member_ref)
        for k in range(2):
            part_ref[lax.rem(me + s, bands), k, :, half * some * channels : (half + 1) * some * channels] = results[k]

    for half, flat in enumerate(norms(1)):
        raise_chunk(flat, half, some, up_ref, act_ref)

    @pl.loop(1, bands)
    def _(s):
        projs = downs()
        flats = norms(s + 1)
        for half in range(halves):
            lower_half(s, half, projs[half])
            raise_chunk(flats[half], half, some, up_ref, act_ref)
        sum_out(s).start()

    for half, proj in enumerate(downs()):
        lower_half(bands, half, proj)

    out_ref[...] = part_ref[me]

    @pl.loop(1, bands)
    def _(s):
        sum_in(s).wait_recv()
        there = lax.rem(me + bands - s, bands)
        out_ref[...] += got_ref[there]

    for copy in small_copies:
        copy.wait_send()

    @pl.loop(0, groups)
    def _(g):
        for copy in bin_copies(g):
            copy.wait_send()

        @pl.loop(1, bands)
        def _(s):
            chunk_out(g, s).wait_send()

    @pl.loop(1, bands)
    def _(s):
        sum_out(s).wait_send()


def on_device(
    spectrum,
    w_freq,
    b_freq,
    dilation,
    w_time,
    b_time,
    w_mix,
    ln_gain,
    w_up,
    b_up,
    w_down,
    b_down,
    epoch_lengths,
):
    channels, bins, frames = spectrum.shape
    groups = channels // SUB
    bands = lax.axis_size("band")
    blocks = lax.axis_size("tm")
    hidden = w_up.shape[1]
    epochs = epoch_lengths.shape[1]
    size = bins * bands * SUB
    some = bins // 2
    bf, f32 = jnp.bfloat16, jnp.float32
    vmem = pltpu.VMEM
    dma = pltpu.SemaphoreType.DMA
    totals = pl.pallas_call(
        functools.partial(kernel, bands, blocks, bins, some),
        out_shape=jax.ShapeDtypeStruct((2, epochs, bins * channels), f32),
        in_specs=[pl.BlockSpec(memory_space=vmem)] * 13,
        out_specs=pl.BlockSpec(memory_space=vmem),
        scratch_shapes=[
            vmem((2, channels * bins, 128), bf),
            vmem((channels * 2, frames), bf),
            vmem((channels * 2, frames), bf),
            vmem((channels * 2, frames), bf),
            vmem((channels * 2, frames), bf),
            vmem((2, 2, channels * 2, 128), bf),
            vmem((bins * SUB, frames + 2 * REACH), f32),
            vmem((groups, bands, bins * SUB, 128), bf),
            vmem((groups, size, 128), bf),
            vmem((size, size), bf),
            vmem((size, groups * 128), f32),
            vmem((bands, 2, epochs, bins * channels), f32),
            vmem((bands, 2, epochs, bins * channels), f32),
            vmem((hidden, channels + 16), bf),
            vmem((channels, 128), f32),
            vmem((channels, 128), f32),
            vmem((epochs, 256), bf),
            vmem((channels, 128), jnp.int32),
            vmem((SUB, 128), jnp.int32),
            vmem((128, 128), bf),
            vmem((groups, bins * SUB, SUB * (bins + 4)), bf),
            vmem((2, hidden, some * 128), bf),
            dma((2, 2)),
            dma((groups, 2, 2)),
            dma((4, 2)),
            dma((groups, bands)),
            dma((groups, bands)),
            dma((groups,)),
            dma((bands,)),
            dma((bands,)),
        ],
        compiler_params=pltpu.CompilerParams(collective_id=0, has_side_effects=True),
        name="whole",
    )(
        spectrum.reshape(channels * bins, frames),
        jnp.transpose(w_freq, (0, 2, 1)),
        b_freq[None],
        dilation[None],
        w_time,
        b_time[None],
        w_mix,
        ln_gain[None],
        w_up,
        b_up[None],
        w_down.T,
        b_down[None],
        epoch_lengths,
    )
    lens = epoch_lengths[0].astype(f32)[:, None]
    return totals[0] / lens, totals[1] / lens


def solution(mesh):
    return jax.shard_map(
        on_device,
        mesh=mesh,
        in_specs=(
            P(None, "band", "tm"),
            P(),
            P(),
            P(),
            P(),
            P(),
            P(),
            P(),
            P(),
            P(),
            P(),
            P(),
            P("tm", None),
        ),
        out_specs=(P("tm", "band"), P("tm", "band")),
        check_vma=False,
    )
```

```python
import functools

import jax
import jax.numpy as jnp
from jax import lax
from jax.experimental import pallas as pl
from jax.experimental.pallas import tpu as pltpu
from jax.sharding import PartitionSpec as P

MESH = pl.DeviceIdType.MESH
REACH = 128
SUB = 8
GELU_C = 0.7978845608028654
GELU_A = 0.044715


def gelu_of_half(h):
    inner = h * (2 * GELU_C + (8 * GELU_C * GELU_A) * (h * h))
    return h + h * jnp.tanh(inner)


def gelu_of_half_narrow(h):
    inner = h * (jnp.bfloat16(2 * GELU_C) + jnp.bfloat16(8 * GELU_C * GELU_A) * (h * h))
    return h + h * jnp.tanh(inner)


def three_parts(value):
    first = value.astype(jnp.bfloat16).astype(jnp.float32)
    second = (value - first).astype(jnp.bfloat16).astype(jnp.float32)
    third = (value - first - second).astype(jnp.bfloat16).astype(jnp.float32)
    return first, second, third


def build_kron(mix_ref, kron_ref):
    size = kron_ref.shape[0]
    bins = size // SUB
    one = (
        lax.broadcasted_iota(jnp.int32, (size, bins), 0) // SUB
        == lax.broadcasted_iota(jnp.int32, (size, bins), 1)
    ).astype(jnp.bfloat16)
    tall = jnp.dot(one, mix_ref[...], preferred_element_type=jnp.float32).astype(jnp.bfloat16)
    wide = (
        lax.broadcasted_iota(jnp.int32, (bins, size), 1) // SUB
        == lax.broadcasted_iota(jnp.int32, (bins, size), 0)
    ).astype(jnp.bfloat16)
    kron_ref[...] = jnp.zeros_like(kron_ref)
    step = 256
    rows = lax.broadcasted_iota(jnp.int32, (step, step), 0)
    cols = lax.broadcasted_iota(jnp.int32, (step, step), 1)
    same = (rows % SUB) == (cols % SUB)
    for i in range(size // step):
        for j in range(size // step):
            part = jnp.dot(
                tall[i * step : (i + 1) * step],
                wide[:, j * step : (j + 1) * step],
                preferred_element_type=jnp.float32,
            )
            kron_ref[i * step : (i + 1) * step, j * step : (j + 1) * step] = jnp.where(
                same, part, 0.0
            ).astype(jnp.bfloat16)


def stacked3(tile, groups, row):
    return jnp.concatenate([tile[g, row * SUB : (row + 1) * SUB, :] for g in range(groups)], axis=0)


def stacked(tile, groups, row):
    return jnp.concatenate(
        [tile[row * SUB : (row + 1) * SUB, g * 128 : (g + 1) * 128] for g in range(groups)], axis=0
    )


def norm_chunk(chunk, some, groups, mixed_ref, gain_ref):
    channels = groups * SUB
    rows = some * SUB
    base = pl.multiple_of(chunk * rows, rows)
    mixed = mixed_ref[pl.ds(base, rows), :]
    normed = []
    for r in range(some):
        m = stacked(mixed, groups, r)
        dev = m - jnp.sum(m, axis=0, keepdims=True) * (1.0 / channels)
        var = jnp.sum(dev * dev, axis=0, keepdims=True) * (1.0 / channels)
        normed.append((dev * lax.rsqrt(var + 1e-05) * gain_ref[...]).astype(jnp.bfloat16))
    flat = jnp.concatenate(normed, axis=1)
    return jnp.concatenate([flat, jnp.ones((16, some * 128), jnp.bfloat16)], axis=0)


def raise_chunk(flat, half, some, up_ref, act_ref):
    hidden = jnp.dot(up_ref[...], flat, preferred_element_type=jnp.float32)
    for r in range(some):
        cols = slice(r * 128, (r + 1) * 128)
        act_ref[half, :, cols] = gelu_of_half_narrow(hidden[:, cols].astype(jnp.bfloat16))


def lower_chunk(chunk, proj, some, groups, data_ref, bdown_ref, member_ref):
    rows = some * SUB
    base = pl.multiple_of(chunk * rows, rows)
    data = data_ref[:, pl.ds(base, rows), :].astype(jnp.float32)
    plain, square = [], []
    for r in range(some):
        block = proj[:, r * 128 : (r + 1) * 128] + bdown_ref[...] + stacked3(data, groups, r)
        for value, store in ((block, plain), (block * block, square)):
            head = value.astype(jnp.bfloat16)
            tail = (value - head.astype(jnp.float32)).astype(jnp.bfloat16)
            store.append(jnp.concatenate([head, tail], axis=1))
    return [
        lax.dot_general(
            member_ref[...],
            jnp.concatenate(store, axis=0),
            (((1,), (1,)), ((), ())),
            preferred_element_type=jnp.float32,
        )
        for store in (plain, square)
    ]


def column(row, first, count):
    lane = lax.broadcasted_iota(jnp.int32, (count, row.shape[1]), 1)
    sub = lax.broadcasted_iota(jnp.int32, (count, row.shape[1]), 0)
    picked = jnp.where(lane == sub + first, jnp.broadcast_to(row, lane.shape), 0.0)
    return jnp.sum(picked, axis=1, keepdims=True)


def wide(col):
    return jnp.broadcast_to(col, (col.shape[0], 128))


def edge_picker(bins):
    shape = (4 * SUB, SUB * bins)
    row = lax.broadcasted_iota(jnp.int32, shape, 0)
    col = lax.broadcasted_iota(jnp.int32, shape, 1)
    edge = row % 2 + jnp.where(row >= 2 * SUB, bins - 2, 0)
    channel = (row % (2 * SUB)) // 2
    return (col == channel * bins + edge).astype(jnp.bfloat16)


def weight_indices(apart_ref, place_ref, order_ref, size, bins, taps, low_on, high_on):
    long = bins + taps - 1
    row = lax.broadcasted_iota(jnp.int32, apart_ref.shape, 0)
    q = lax.broadcasted_iota(jnp.int32, apart_ref.shape, 1)
    apart_ref[...] = jnp.where(q < size * long, row - q // long, -4096)
    place_ref[...] = lax.broadcasted_iota(jnp.int32, place_ref.shape, 1) % long
    p = lax.broadcasted_iota(jnp.int32, order_ref.shape, 1)
    src = lax.broadcasted_iota(jnp.int32, order_ref.shape, 0)
    inner = size * bins
    lo = p - inner
    hi = lo - 2 * size
    wanted = jnp.where(
        p < inner,
        (p // bins) * long + p % bins + 2,
        jnp.where(
            lo < 2 * size,
            (lo // 2) * long + lo % 2 + jnp.where(low_on, 0, 4096),
            (hi // 2) * long + bins + 2 + hi % 2 + jnp.where(high_on, 0, 4096),
        ),
    )
    order_ref[...] = ((src == wanted) & (p < size * long)).astype(jnp.bfloat16)


def group_weights(wt_ref, g, bins, apart_ref, place_ref, order_ref):
    taps, size, channels = wt_ref.shape
    wid = size * (bins + taps - 1)
    pick = (apart_ref[...] == g * size).astype(jnp.bfloat16)
    place = place_ref[...]
    base = jnp.zeros((size, 128), jnp.float32)
    for k in range(taps):
        spread = jnp.dot(wt_ref[k], pick, preferred_element_type=jnp.float32)
        base = jnp.where(place == k, spread, base)
    base = 0.5 * base
    turned = [base] + [pltpu.roll(base, f, 1) for f in range(1, bins)]
    big = jnp.concatenate(turned, axis=0).astype(jnp.bfloat16)
    ready = jnp.dot(big, order_ref[...], preferred_element_type=jnp.float32)
    return ready[:, :wid].astype(jnp.bfloat16)


def front_group(g, bands, weights, own_ref, ends_ref, low_ref, high_ref, cor_ref, rows_of, before_on, after_on, spec_ref, send_ref):
    rows = weights.shape[0]
    long = own_ref.shape[1]
    t0, t1, t2, shift, bias8, step = (wide(column(r, g * SUB, SUB)) for r in rows_of)
    bias = jnp.concatenate([0.5 * bias8] * (rows // SUB), axis=0)
    tiles = long // 128 + 2
    at = pl.multiple_of(g * rows, rows)
    small = pl.multiple_of(g * 16, 16)
    body = jnp.concatenate(
        [own_ref[pl.ds(at, rows), :], low_ref[pl.ds(small, 16), :], high_ref[pl.ds(small, 16), :]],
        axis=0,
    )
    first, last = (
        jnp.concatenate(
            [
                ends_ref[i, pl.ds(at, rows), :],
                cor_ref[i, 0, pl.ds(small, 16), :],
                cor_ref[i, 1, pl.ds(small, 16), :],
            ],
            axis=0,
        )
        for i in range(2)
    )
    data = jnp.concatenate([first, body, last], axis=1)
    pre = jnp.dot(weights, data, preferred_element_type=jnp.float32)
    step = step.astype(jnp.int32)
    for j in range(tiles):
        cols = slice(j * 128, (j + 1) * 128)
        act = gelu_of_half(pre[:, cols] + bias)
        if j == 0:
            act = act * before_on
        if j == tiles - 1:
            act = act * after_on
        spec_ref[:, cols] = act.astype(jnp.bfloat16).astype(jnp.float32)
    lane = lax.broadcasted_iota(jnp.int32, (SUB, 128), 1)
    from_left = (lane - step) & 127
    from_right = (lane + step) & 127
    keep_left = lane >= step
    keep_right = lane + step < 128

    def take(value, index):
        return jnp.take_along_axis(value, index, axis=1, mode="promise_in_bounds")

    def half(start):
        v = [spec_ref[start : start + SUB, j * 128 : (j + 1) * 128] for j in range(tiles)]
        left = [take(v[j], from_left) for j in range(tiles - 1)]
        right = [take(v[j], from_right) for j in range(1, tiles)]
        outs = []
        for j in range(1, tiles - 1):
            a = jnp.where(keep_left, left[j], left[j - 1])
            c = jnp.where(keep_right, right[j - 1], right[j])
            outs.append(t0 * a + t1 * v[j] + t2 * c + shift)
        return outs

    for pair in range(rows // 16):
        top = half(pair * 16)
        bottom = half(pair * 16 + SUB)
        for j in range(bands):
            both = jnp.concatenate([top[j], bottom[j]], axis=0)
            send_ref[g, j, pair * 16 : (pair + 1) * 16, :] = both.astype(jnp.bfloat16)


def kernel(
    bands,
    blocks,
    bins,
    some,
    own_ref,
    wt_ref,
    bfreq_ref,
    dil_ref,
    wtime_ref,
    btime_ref,
    mix_ref,
    gain_in,
    up_in,
    bup_in,
    down_ref,
    bdown_in,
    lens_ref,
    out_ref,
    ends_ref,
    plow_ref,
    phigh_ref,
    low_ref,
    high_ref,
    cor_ref,
    spec_ref,
    send_ref,
    data_ref,
    kron_ref,
    mixed_ref,
    part_ref,
    got_ref,
    up_ref,
    bdown_ref,
    gain_ref,
    member_ref,
    apart_ref,
    place_ref,
    order_ref,
    wall_ref,
    act_ref,
    frame_sem,
    bin_sem,
    corner_sem,
    chunk_send,
    chunk_recv,
    local_sem,
    sum_send,
    sum_recv,
):
    me = lax.axis_index("band")
    tm = lax.axis_index("tm")
    channels = wt_ref.shape[2]
    groups = channels // SUB
    frames = own_ref.shape[1]
    rows = bins * SUB
    size = kron_ref.shape[0]

    def around(value, count):
        return lax.rem(value + count, count)

    up_tm, down_tm = around(tm + 1, blocks), around(tm - 1, blocks)
    up_band, down_band = around(me + 1, bands), around(me - 1, bands)

    barrier = pltpu.get_barrier_semaphore()

    @pl.loop(1, bands)
    def _(s):
        pl.semaphore_signal(barrier, inc=1, device_id={"band": lax.rem(me + s, bands), "tm": tm}, device_id_type=MESH)

    for t in (up_tm, down_tm):
        for b in (me, up_band, down_band):
            pl.semaphore_signal(barrier, inc=1, device_id={"band": b, "tm": t}, device_id_type=MESH)
    picker = edge_picker(bins)

    @pl.loop(0, groups)
    def _(g):
        at = pl.multiple_of(g * rows, rows)
        small = pl.multiple_of(g * 16, 16)
        edges = jnp.dot(picker, own_ref[pl.ds(at, rows), :], preferred_element_type=jnp.float32)
        plow_ref[pl.ds(small, 16), :] = edges[:16].astype(jnp.bfloat16)
        phigh_ref[pl.ds(small, 16), :] = edges[16:].astype(jnp.bfloat16)

    pl.semaphore_wait(barrier, bands - 1 + 6)

    def remote(src, dst, send, recv, band, block):
        return pltpu.make_async_remote_copy(
            src_ref=src,
            dst_ref=dst,
            send_sem=send,
            recv_sem=recv,
            device_id={"band": band, "tm": block},
            device_id_type=MESH,
        )

    begin, finish = pl.ds(0, 128), pl.ds(frames - 128, 128)
    small_copies = [
        remote(own_ref.at[:, finish], ends_ref.at[0], frame_sem.at[0, 0], frame_sem.at[0, 1], me, up_tm),
        remote(own_ref.at[:, begin], ends_ref.at[1], frame_sem.at[1, 0], frame_sem.at[1, 1], me, down_tm),
    ]
    k = 0
    for i, (lanes, block) in enumerate(((finish, up_tm), (begin, down_tm))):
        for h, (pack, band) in enumerate(((phigh_ref, up_band), (plow_ref, down_band))):
            small_copies.append(
                remote(pack.at[:, lanes], cor_ref.at[i, h], corner_sem.at[k, 0], corner_sem.at[k, 1], band, block)
            )
            k += 1

    def bin_copies(g):
        span = pl.ds(pl.multiple_of(g * 16, 16), 16)
        return (
            remote(phigh_ref.at[span, :], low_ref.at[span, :], bin_sem.at[g, 0, 0], bin_sem.at[g, 0, 1], up_band, tm),
            remote(plow_ref.at[span, :], high_ref.at[span, :], bin_sem.at[g, 1, 0], bin_sem.at[g, 1, 1], down_band, tm),
        )

    for copy in small_copies:
        copy.start()

    @pl.loop(0, groups)
    def _(g):
        for copy in bin_copies(g):
            copy.start()

    def chunk_out(g, s):
        there = lax.rem(me + s, bands)
        place = pl.ds(pl.multiple_of(me * rows, rows), rows)
        return remote(send_ref.at[g, there], data_ref.at[g, place, :], chunk_send.at[g, s], chunk_recv.at[g, s], there, tm)

    def chunk_in(g, s):
        there = lax.rem(me + bands - s, bands)
        place = pl.ds(pl.multiple_of(there * rows, rows), rows)
        return remote(send_ref.at[g, there], data_ref.at[g, place, :], chunk_send.at[g, s], chunk_recv.at[g, s], there, tm)

    def chunk_here(g):
        place = pl.ds(pl.multiple_of(me * rows, rows), rows)
        return pltpu.make_async_copy(send_ref.at[g, me], data_ref.at[g, place, :], local_sem.at[g])

    before_on = jnp.where(tm > 0, 1.0, 0.0).astype(jnp.float32)
    after_on = jnp.where(tm < blocks - 1, 1.0, 0.0).astype(jnp.float32)
    rows_of = (
        wtime_ref[0:1],
        wtime_ref[1:2],
        wtime_ref[2:3],
        btime_ref[...],
        bfreq_ref[...],
        dil_ref[...].astype(jnp.float32),
    )
    weight_indices(apart_ref, place_ref, order_ref, SUB, bins, wt_ref.shape[0], me > 0, me < bands - 1)

    @pl.loop(0, groups)
    def _(g):
        wall_ref[g] = group_weights(wt_ref, g, bins, apart_ref, place_ref, order_ref)

    sub = lax.broadcasted_iota(jnp.int32, (16, up_in.shape[1]), 0)
    extra = jnp.zeros(sub.shape, jnp.float32)
    for i, piece in enumerate(three_parts(bup_in[...])):
        extra = jnp.where(sub == i, piece, extra)
    tall = 0.5 * jnp.concatenate([up_in[...].astype(jnp.float32), extra], axis=0)
    up_ref[...] = tall.T.astype(jnp.bfloat16)
    bdown_ref[...] = wide(column(bdown_in[...], 0, channels))
    gain_ref[...] = wide(column(gain_in[...], 0, channels))
    lens = lens_ref[...].astype(jnp.float32)
    epochs = lens.shape[1]
    eye_r = lax.broadcasted_iota(jnp.int32, (epochs, epochs), 0)
    eye_c = lax.broadcasted_iota(jnp.int32, (epochs, epochs), 1)
    all_lens = jnp.broadcast_to(lens, (epochs, epochs))
    own_len = jnp.sum(jnp.where(eye_r == eye_c, all_lens, 0.0), axis=1, keepdims=True)
    starts = jnp.sum(jnp.where(eye_c < eye_r, all_lens, 0.0), axis=1, keepdims=True)
    ids = (me * 128 + lax.broadcasted_iota(jnp.int32, (epochs, 128), 1)).astype(jnp.float32)
    member = jnp.where((ids >= starts) & (ids < starts + own_len), 1.0, 0.0)
    member_ref[...] = jnp.concatenate([member, member], axis=1).astype(jnp.bfloat16)

    for copy in small_copies:
        copy.wait_recv()

    @pl.loop(0, groups)
    def _(g):
        for copy in bin_copies(g):
            copy.wait_recv()
        front_group(g, bands, wall_ref[g], own_ref, ends_ref, low_ref, high_ref, cor_ref, rows_of, before_on, after_on, spec_ref, send_ref)

        @pl.loop(1, bands)
        def _(k):
            step = (k // 2) * (2 * (k % 2) - 1)
            chunk_out(g, bands // 2 + step).start()

        chunk_here(g).start()

    build_kron(mix_ref, kron_ref)

    @pl.loop(0, groups // 2)
    def _(p):
        for g in (2 * p, 2 * p + 1):
            chunk_here(g).wait()

            @pl.loop(1, bands)
            def _(s):
                chunk_in(g, s).wait_recv()

        cols = pl.ds(pl.multiple_of(p * 256, 256), 256)
        both = jnp.concatenate([data_ref[2 * p], data_ref[2 * p + 1]], axis=1)
        step = 256
        for i in range(size // step):
            mixed_ref[i * step : (i + 1) * step, cols] = jnp.dot(
                kron_ref[i * step : (i + 1) * step, :], both, preferred_element_type=jnp.float32
            )

    def sum_out(s):
        there = lax.rem(me + s, bands)
        return remote(part_ref.at[there], got_ref.at[me], sum_send.at[s], sum_recv.at[s], there, tm)

    def sum_in(s):
        there = lax.rem(me + bands - s, bands)
        return remote(part_ref.at[there], got_ref.at[there], sum_send.at[s], sum_recv.at[s], there, tm)

    halves = bins // some

    def chunk_of(s, half):
        return lax.rem(me + s, bands) * halves + half

    def norms(s):
        return [norm_chunk(chunk_of(s, half), some, groups, mixed_ref, gain_ref) for half in range(halves)]

    def downs():
        return [
            jnp.dot(down_ref[...], act_ref[half], preferred_element_type=jnp.float32)
            for half in range(halves)
        ]

    def lower_half(s, half, proj):
        results = lower_chunk(chunk_of(s, half), proj, some, groups, data_ref, bdown_ref, member_ref)
        for k in range(2):
            part_ref[lax.rem(me + s, bands), k, :, half * some * channels : (half + 1) * some * channels] = results[k]

    for half, flat in enumerate(norms(1)):
        raise_chunk(flat, half, some, up_ref, act_ref)

    @pl.loop(1, bands)
    def _(s):
        projs = downs()
        flats = norms(s + 1)
        for half in range(halves):
            lower_half(s, half, projs[half])
            raise_chunk(flats[half], half, some, up_ref, act_ref)
        sum_out(s).start()

    for half, proj in enumerate(downs()):
        lower_half(bands, half, proj)

    out_ref[...] = part_ref[me]

    @pl.loop(1, bands)
    def _(s):
        sum_in(s).wait_recv()
        there = lax.rem(me + bands - s, bands)
        out_ref[...] += got_ref[there]

    out_ref[...] = out_ref[...] / own_len

    for copy in small_copies:
        copy.wait_send()

    @pl.loop(0, groups)
    def _(g):
        for copy in bin_copies(g):
            copy.wait_send()

        @pl.loop(1, bands)
        def _(s):
            chunk_out(g, s).wait_send()

    @pl.loop(1, bands)
    def _(s):
        sum_out(s).wait_send()


def on_device(
    spectrum,
    w_freq,
    b_freq,
    dilation,
    w_time,
    b_time,
    w_mix,
    ln_gain,
    w_up,
    b_up,
    w_down,
    b_down,
    epoch_lengths,
):
    channels, bins, frames = spectrum.shape
    groups = channels // SUB
    bands = lax.axis_size("band")
    blocks = lax.axis_size("tm")
    hidden = w_up.shape[1]
    epochs = epoch_lengths.shape[1]
    size = bins * bands * SUB
    some = bins // 2
    bf, f32 = jnp.bfloat16, jnp.float32
    vmem = pltpu.VMEM
    dma = pltpu.SemaphoreType.DMA
    totals = pl.pallas_call(
        functools.partial(kernel, bands, blocks, bins, some),
        out_shape=jax.ShapeDtypeStruct((2, epochs, bins * channels), f32),
        in_specs=[pl.BlockSpec(memory_space=vmem)] * 13,
        out_specs=pl.BlockSpec(memory_space=vmem),
        scratch_shapes=[
            vmem((2, channels * bins, 128), bf),
            vmem((channels * 2, frames), bf),
            vmem((channels * 2, frames), bf),
            vmem((channels * 2, frames), bf),
            vmem((channels * 2, frames), bf),
            vmem((2, 2, channels * 2, 128), bf),
            vmem((bins * SUB, frames + 2 * REACH), f32),
            vmem((groups, bands, bins * SUB, 128), bf),
            vmem((groups, size, 128), bf),
            vmem((size, size), bf),
            vmem((size, groups * 128), f32),
            vmem((bands, 2, epochs, bins * channels), f32),
            vmem((bands, 2, epochs, bins * channels), f32),
            vmem((hidden, channels + 16), bf),
            vmem((channels, 128), f32),
            vmem((channels, 128), f32),
            vmem((epochs, 256), bf),
            vmem((channels, 128), jnp.int32),
            vmem((SUB, 128), jnp.int32),
            vmem((128, 128), bf),
            vmem((groups, bins * SUB, SUB * (bins + 4)), bf),
            vmem((2, hidden, some * 128), bf),
            dma((2, 2)),
            dma((groups, 2, 2)),
            dma((4, 2)),
            dma((groups, bands)),
            dma((groups, bands)),
            dma((groups,)),
            dma((bands,)),
            dma((bands,)),
        ],
        compiler_params=pltpu.CompilerParams(collective_id=0, has_side_effects=True),
        name="whole",
    )(
        spectrum.reshape(channels * bins, frames),
        jnp.transpose(w_freq, (0, 2, 1)),
        b_freq[None],
        dilation[None],
        w_time,
        b_time[None],
        w_mix,
        ln_gain[None],
        w_up,
        b_up[None],
        w_down.T,
        b_down[None],
        epoch_lengths,
    )
    return totals[0], totals[1]


def solution(mesh):
    return jax.shard_map(
        on_device,
        mesh=mesh,
        in_specs=(
            P(None, "band", "tm"),
            P(),
            P(),
            P(),
            P(),
            P(),
            P(),
            P(),
            P(),
            P(),
            P(),
            P(),
            P("tm", None),
        ),
        out_specs=(P("tm", "band"), P("tm", "band")),
        check_vma=False,
    )
```
